32 devices in a mesh: row: 4 (over z), col: 8 (over y, x, core).
Axes of the slice: x: 2, y: 2, z: 4, core: 2. Of those that a mesh axis runs over, the one named last changes fastest.
Arguments:
- frames: float32 [512, 64, 1024], P(('row', 'col')), may hold values from -1 to 6
- class_index: int32 [64, 1024], P('row', 'col'), may hold values from 0 to 7
- surface_mask: int32 [64, 1024], P('row', 'col'), may hold values 0 or 1
- effusivity: float32 [8], replicated, may hold values from 0.5 to 2
- conductivity: float32 [8], replicated, may hold values from 0.2 to 1
Outputs:
- heat_flux: float32 [64, 1024, 512], P('row', 'col')
The draws below stay inside these ranges and needn't reach their ends.
All inputs are finite; a program needn't handle non-finite values. No bound on the sum of `surface_mask` on one device may be relied on, other than what follows from the above.
Results may differ from the reference program's by a relative error of at most 0.0003.
Values sent between devices are 32-bit elements; how exact they have to be, the bound alone decides.
A program may use at most 64 MiB of HBM per device.

```python
import math
import jax
import jax.numpy as jnp
from jax import lax

FRAMES = 512
NCLASS = 8
PASSES = 3
HEIGHT = 64
WIDTH = 1024


def draw_frames(key, part):
    amp_key = jax.random.fold_in(key, 11)
    onset_key = jax.random.fold_in(key, 23)
    noise_key = jax.random.fold_in(key, 37)
    amplitude = jnp.exp(jax.random.uniform(amp_key, (HEIGHT, WIDTH), jnp.float32, math.log(0.5), math.log(5.0)))
    onset = jax.random.randint(onset_key, (HEIGHT, WIDTH), 0, FRAMES // 2).astype(jnp.float32)
    times = jnp.arange(FRAMES, dtype=jnp.float32)[:, None, None]
    elapsed = jnp.maximum(times - onset[None], 0.0)
    started = jnp.where(times >= onset[None], 1.0, 0.0)
    ramp = jnp.sqrt(elapsed / (FRAMES - onset[None]))
    noise = 0.05 * jax.random.normal(noise_key, (FRAMES, HEIGHT, WIDTH), jnp.float32)
    jump_share = 0.3
    ramp_share = 0.6
    history = amplitude[None] * (ramp_share * ramp + jump_share * started + noise)
    return jnp.clip(history, -1.0, 6.0)


def plant(array, stream_key, low, top_value):
    index_at = [jax.random.randint(jax.random.fold_in(stream_key, axis), (), 0, length) for axis, length in enumerate(array.shape)]
    longest = array.shape.index(max(array.shape))
    neighbour = index_at[:longest] + [(index_at[longest] + 1) % array.shape[longest]] + index_at[longest + 1:]
    return array.at[tuple(index_at)].set(low).at[tuple(neighbour)].set(top_value)


def setup_inputs(seed: int = 0) -> dict:
    key_of = jax.random.split(jax.random.key(seed), 6)
    frames = draw_frames(jax.random.fold_in(key_of[5], 71), 0)
    class_index = plant(jax.random.randint(key_of[1], (HEIGHT, WIDTH), 0, NCLASS), jax.random.fold_in(key_of[1], 1), 0, NCLASS - 1).astype(jnp.int32)
    surface_mask = plant((jax.random.randint(key_of[2], (HEIGHT, WIDTH), 0, 4) < 3).astype(jnp.int32), jax.random.fold_in(key_of[2], 1), 0, 1)
    effusivity = jnp.clip(jnp.exp(jax.random.uniform(key_of[3], (NCLASS,), jnp.float32, math.log(0.5), math.log(2.0))), 0.5, 2.0)
    conductivity = jnp.clip(jnp.exp(jax.random.uniform(key_of[4], (NCLASS,), jnp.float32, math.log(0.2), math.log(1.0))), 0.2, 1.0)
    return dict(frames=frames, class_index=class_index, surface_mask=surface_mask, effusivity=effusivity, conductivity=conductivity)


flux_factor = 1.1283791670955126
lateral_rate = 0.24

def weights(lagged):
    clipped = jnp.maximum(lagged, 0.0)
    return jnp.where(lagged >= 0.0, 1.0 / (jnp.sqrt(clipped) + jnp.sqrt(clipped + 1.0)), 0.0)

def kernel_from(later, earlier):
    lagged = (later[:, None] - earlier[None, :]).astype(jnp.float32)
    return weights(lagged) - weights(lagged - 1.0)

def reference(frames, class_index, surface_mask, effusivity, conductivity):
    frame_ids = jnp.arange(FRAMES, dtype=jnp.int32)
    kernel = kernel_from(frame_ids, frame_ids)
    convolved = lax.dot_general(frames, kernel, (((0,), (1,)), ((), ())), precision=lax.Precision.HIGHEST)
    maskf = surface_mask.astype(jnp.float32)
    gain = flux_factor * effusivity[class_index] * maskf
    lateral = lateral_rate * conductivity[class_index] * maskf
    heat_flux = convolved * gain[:, :, None]
    for pass_index in range(PASSES):
        padded = jnp.pad(heat_flux, ((1, 1), (1, 1), (0, 0)))
        center = padded[1:-1, 1:-1]
        laplace = padded[2:, 1:-1] + padded[:-2, 1:-1] + padded[1:-1, 2:] + padded[1:-1, :-2] - 4.0 * center
        heat_flux = center + lateral[:, :, None] * laplace
    return heat_flux
```

```python
import functools
import jax
import jax.numpy as jnp
from jax import lax
from jax.experimental import pallas as pl
from jax.experimental.pallas import tpu as pltpu
from jax.sharding import PartitionSpec as P

PASSES = 3
PAD = 8
GROUP = 8
LANES = 128
STEPS = 8
VMEM_GATHER = 40 * 2**20
MESH = pl.DeviceIdType.MESH

flux_factor = 1.1283791670955126
lateral_rate = 0.24


def extended(block, sides, width):
    for axis, dim in sides:
        count = lax.axis_size(axis)
        forward = [(i, i + 1) for i in range(count - 1)]
        backward = [(target, source) for source, target in forward]
        low = lax.ppermute(
            lax.slice_in_dim(block, block.shape[dim] - width, None, axis=dim), axis, forward
        )
        high = lax.ppermute(lax.slice_in_dim(block, 0, width, axis=dim), axis, backward)
        block = jnp.concatenate([low, block, high], axis=dim)
    return block


def weights(lagged):
    clipped = jnp.maximum(lagged, 0.0)
    return jnp.where(lagged >= 0.0, 1.0 / (jnp.sqrt(clipped) + jnp.sqrt(clipped + 1.0)), 0.0)


def kernel_from(later, earlier):
    lagged = (later[:, None] - earlier[None, :]).astype(jnp.float32)
    return weights(lagged) - weights(lagged - 1.0)


def relax_once(padded, lateral):
    center = padded[1:-1, 1:-1]
    laplace = (
        padded[2:, 1:-1] + padded[:-2, 1:-1] + padded[1:-1, 2:] + padded[1:-1, :-2] - 4.0 * center
    )
    return center + lateral[:, :, None] * laplace


def plain_device(frames, class_index, surface_mask, effusivity, conductivity):
    row_count = lax.axis_size("row")
    col_count = lax.axis_size("col")
    local_frames, height, width = frames.shape
    tile_rows = height // row_count
    tile_cols = width // col_count
    total_frames = local_frames * row_count * col_count
    frame_ids = jnp.arange(total_frames, dtype=jnp.int32)
    contract = (((0,), (1,)), ((), ()))
    kernel = kernel_from(frame_ids, frame_ids)
    blocks = frames.reshape(local_frames, row_count, tile_rows, col_count, tile_cols)
    blocks = blocks.transpose(0, 1, 3, 2, 4).reshape(
        local_frames, row_count * col_count, tile_rows, tile_cols
    )
    convolved = lax.dot_general(
        lax.all_to_all(blocks, ("row", "col"), split_axis=1, concat_axis=0, tiled=True)[:, 0],
        kernel,
        contract,
        precision=lax.Precision.HIGHEST,
    )
    classes = jnp.arange(effusivity.shape[0], dtype=jnp.int32)
    matches = (class_index[:, :, None] == classes[None, None, :]).astype(jnp.float32)
    maskf = surface_mask.astype(jnp.float32)
    gain = flux_factor * jnp.sum(matches * effusivity, axis=-1) * maskf
    lateral = lateral_rate * jnp.sum(matches * conductivity, axis=-1) * maskf
    heat_flux = convolved * gain[:, :, None]
    padded = extended(heat_flux, (("row", 0), ("col", 1)), PASSES)
    lateral_wide = extended(lateral, (("row", 0), ("col", 1)), PASSES - 1)
    for pass_index in range(PASSES):
        margin = PASSES - 1 - pass_index
        offset = PASSES - 1 - margin
        lateral_part = lateral_wide[
            offset : offset + tile_rows + 2 * margin, offset : offset + tile_cols + 2 * margin
        ]
        padded = relax_once(padded, lateral_part)
    return padded


def gather_kernel(
    rows, cols, tile_rows, tile_cols, local, height, steps,
    frames, class_in, mask_in, eff_in, cond_in,
    held, flux, mix_ref,
    x, coef, done, done_far, first, second, edge_out, edge_in,
    class_ref, mask_ref, eff_ref, cond_ref,
    load_sem, small_sem, coef_send, near_recv, pair_recv, far_recv,
    raw_send, raw_recv, edge_send, edge_recv,
    near_send, cross_send, relay_send, recv_sem,
):
    row, col = lax.axis_index("row"), lax.axis_index("col")
    mid = rows // 2
    half = row // mid
    other = 1 - half
    half_rows = height // 2
    total = rows * cols * local
    halo = PASSES
    near = mid * cols - 1
    part = tile_rows // steps
    source = row * cols + col
    mirror, pair = rows - 1 - row, lax.rem(row + mid, rows)
    raw = ((row == mid - 1) | (row == mid)) & (lax.rem(col, 2) == 0)

    def wait_for(ref, sem):
        pltpu.make_async_copy(ref, ref, sem).wait()

    def aligned(value, unit):
        return pl.multiple_of(value, unit)

    def remote(src, dst, send, recv, to_row, to_col):
        return pltpu.make_async_remote_copy(
            src_ref=src, dst_ref=dst, send_sem=send, recv_sem=recv,
            device_id=(to_row, to_col), device_id_type=MESH,
        )

    def in_half(i):
        at = lax.rem(row * cols + col - half * (near + 1) + i, near + 1)
        return half * mid + at // cols, lax.rem(at, cols)

    smalls = [
        pltpu.make_async_copy(src, dst, small_sem.at[i])
        for i, (src, dst) in enumerate(
            ((class_in, class_ref), (mask_in, mask_ref), (eff_in, eff_ref), (cond_in, cond_ref))
        )
    ]
    for copy in smalls:
        copy.start()
    for c in range(cols):
        pltpu.make_async_copy(
            frames.at[:, :, c * LANES : (c + 1) * LANES], x.at[c, 0:local], load_sem
        ).start()

    barrier = pltpu.get_barrier_semaphore()

    @pl.when(raw)
    def _():
        pl.semaphore_signal(barrier, inc=1, device_id=(mirror, col), device_id_type=MESH)

    pl.semaphore_signal(barrier, inc=1, device_id=(pair, col), device_id_type=MESH)

    @pl.loop(1, near + 1)
    def _(i):
        pl.semaphore_signal(barrier, inc=1, device_id=in_half(i), device_id_type=MESH)

    for copy in smalls:
        copy.wait()
    classes = class_ref[...]
    maskf = mask_ref[...].astype(jnp.float32)
    eff = jnp.zeros(classes.shape, jnp.float32)
    cond = jnp.zeros(classes.shape, jnp.float32)
    for k in range(eff_ref.shape[0]):
        eff = jnp.where(classes == k, eff_ref[k], eff)
        cond = jnp.where(classes == k, cond_ref[k], cond)

    def tile_of(at_row, at_col):
        return coef.at[at_col, :, pl.ds(aligned(PAD + at_row * tile_rows, PAD), tile_rows)]

    own_rows = pl.ds(aligned(PAD + row * tile_rows, PAD), tile_rows)
    coef[col, 0, own_rows] = lateral_rate * cond * maskf
    coef[col, 1, own_rows] = flux_factor * eff * maskf
    for c in range(cols):
        for k in range(2):
            coef[c, k, 0:PAD] = jnp.zeros((PAD, LANES), jnp.float32)
            coef[c, k, PAD + height : 2 * PAD + height] = jnp.zeros((PAD, LANES), jnp.float32)

    pl.semaphore_wait(barrier, near + 1 + raw.astype(jnp.int32))

    own_tile, pair_tile = tile_of(row, col), tile_of(pair, col)
    remote(own_tile, own_tile, coef_send.at[0], pair_recv, pair, col).start()

    @pl.loop(1, near + 1)
    def _(i):
        to_row, to_col = in_half(i)
        remote(own_tile, own_tile, coef_send.at[1], near_recv, to_row, to_col).start()

    far_rows = pl.ds(aligned(other * half_rows, PAD), half_rows)
    near_rows = pl.ds(aligned(half * half_rows, PAD), half_rows)

    def raw_copy(c):
        return remote(
            frames.at[0:GROUP, far_rows, c * LANES : (c + 1) * LANES],
            x.at[c, local : local + GROUP, far_rows],
            raw_send, raw_recv, mirror, col,
        )

    edge_copy = remote(edge_out, edge_in, edge_send, edge_recv, mirror, col)

    @pl.when(raw)
    def _():
        for c in range(cols):
            raw_copy(c).start()

    wait_for(x.at[:, 0:local], load_sem)
    lines = x.reshape(cols, (local + GROUP) * height, LANES)

    def line(c, group, at):
        return lines[c, pl.ds(group * (GROUP * height) + at, GROUP, stride=height), :]

    @pl.when(raw)
    def _():
        for k in range(halo):
            for c in range(cols):
                edge_out[k, c] = line(c, 0, half_rows - halo * other + k)
        edge_copy.start()

    def fill_mix():
        block = tile_cols

        @pl.loop(0, total // block)
        def _(k):
            shape = (block, total)
            earlier = lax.broadcasted_iota(jnp.int32, shape, 0) + k * block
            later = lax.broadcasted_iota(jnp.int32, shape, 1)
            lagged = (later - earlier).astype(jnp.float32)
            mix = weights(lagged) - weights(lagged - 1.0)
            high = mix.astype(jnp.bfloat16)
            at = pl.ds(aligned(k * block, block), block)
            mix_ref[0, at] = high
            mix_ref[1, at] = (mix - high.astype(jnp.float32)).astype(jnp.bfloat16)

    lane = lax.broadcasted_iota(jnp.int32, (GROUP, LANES), 1)
    leftmost, rightmost = lane == 0, lane == LANES - 1
    nothing = jnp.zeros((GROUP, LANES), jnp.float32)

    def spread(c, which, at):
        return coef[c, which, pl.ds(at, GROUP, stride=0), :]

    def clear(side):
        for k in range(halo):
            for c in range(cols):
                first[(half_rows + halo) * side + k, c] = nothing

    def relax(source_ref, side, begin, end, store):
        base = side * half_rows - halo + PAD

        @pl.loop(begin, end)
        def _(i):
            center = [source_ref[i, c] for c in range(cols)]
            ahead = [pltpu.roll(v, 1, 1) for v in center]
            behind = [pltpu.roll(v, LANES - 1, 1) for v in center]
            for c in range(cols):
                left = jnp.where(leftmost, ahead[c - 1] if c else nothing, ahead[c])
                right = jnp.where(rightmost, behind[c + 1] if c + 1 < cols else nothing, behind[c])
                laplace = source_ref[i + 1, c] + source_ref[i - 1, c] + right + left - 4.0 * center[c]
                store(i, c, center[c] + spread(c, 0, base + i) * laplace)

    def passes(side, store_last):
        def keep(ref):
            def store(i, c, value):
                ref[i, c] = value
            return store

        span = half_rows + 2 * halo
        relax(first, side, 1, span - 1, keep(second))
        relax(second, side, 2, span - 2, keep(first))
        relax(first, side, halo, span - halo, store_last)

    def sweep(side, group):
        clear(side)

        @pl.loop(0, half_rows + halo)
        def _(k):
            at = (half_rows - halo) * side + k
            for c in range(cols):
                first[halo * (1 - side) + k, c] = spread(c, 1, at + PAD) * line(c, group, at)

        def store(i, c, value):
            j = i - halo
            at = pl.ds(aligned(group * GROUP, GROUP), GROUP)
            done[side * mid + j // tile_rows, c, lax.rem(j, tile_rows), at, :] = value

        passes(side, store)

    def sweep_raw():
        clear(half)

        @pl.loop(0, half_rows)
        def _(k):
            at = half_rows * half + k
            for c in range(cols):
                first[halo + k, c] = spread(c, 1, at + PAD) * line(c, local // GROUP, at)

        for k in range(halo):
            for c in range(cols):
                at = half_rows - halo * half + k
                first[(half_rows + halo) * (1 - half) + k, c] = spread(c, 1, at + PAD) * edge_in[k, c]

        def store(i, c, value):
            j = i - halo
            done_far[j // tile_rows, c, lax.rem(j, tile_rows), :, :] = value

        passes(half, store)

    groups = local // GROUP

    def rows_of(q):
        return pl.ds(q * part, part)

    def slots(at, count):
        return pl.ds(aligned(at, GROUP), count)

    fill_mix()

    wait_for(pair_tile, pair_recv)

    @pl.loop(1, near + 1)
    def _(i):
        to_row, to_col = in_half(i)
        remote(pair_tile, pair_tile, coef_send.at[2], far_recv, to_row, to_col).start()

    def tiles(count):
        return held.at[pl.ds(0, count), pl.ds(0, 2 * tile_rows)]

    wait_for(tiles(near), near_recv)
    wait_for(tiles(near), far_recv)

    @pl.loop(0, groups)
    def _(g):
        sweep(half, g)

    own_slots = slots(source * local, local)

    def near_copy(q, i):
        to_row, to_col = in_half(i)
        return remote(
            done.at[to_row, to_col, rows_of(q)], held.at[rows_of(q), own_slots],
            near_send, recv_sem.at[q], to_row, to_col,
        )

    @pl.loop(0, steps)
    def _(q):
        pltpu.make_async_copy(
            done.at[row, col, rows_of(q)], held.at[rows_of(q), own_slots], recv_sem.at[q]
        ).start()

        @pl.loop(1, near + 1)
        def _(i):
            near_copy(q, i).start()

    @pl.loop(raw.astype(jnp.int32), groups)
    def _(g):
        sweep(other, g)

    def across(i):
        at = lax.rem(row * cols + col - half * (near + 1) + i, near + 1)
        return other * mid + at // cols, lax.rem(at, cols)

    def start_cross(skip):
        count = local - skip

        @pl.loop(0, steps)
        def _(q):
            @pl.loop(0, near + 1)
            def _(i):
                to_row, to_col = across(i)
                remote(
                    done.at[to_row, to_col, rows_of(q), pl.ds(skip, count)],
                    held.at[rows_of(q), slots(source * local + skip, count)],
                    cross_send, recv_sem.at[q], to_row, to_col,
                ).start()

    @pl.when(raw)
    def _():
        start_cross(GROUP)

    @pl.when(jnp.logical_not(raw))
    def _():
        start_cross(0)

    @pl.when(raw)
    def _():
        wait_for(x.at[:, local : local + GROUP, near_rows], raw_recv)
        edge_copy.wait_recv()
        sweep_raw()
        there = slots((mirror * cols + col) * local, GROUP)

        @pl.loop(0, steps)
        def _(q):
            pltpu.make_async_copy(
                done_far.at[row - half * mid, col, rows_of(q)], held.at[rows_of(q), there],
                recv_sem.at[q],
            ).start()

            @pl.loop(1, near + 1)
            def _(i):
                to_row, to_col = in_half(i)
                remote(
                    done_far.at[to_row - half * mid, to_col, rows_of(q)],
                    held.at[rows_of(q), there],
                    relay_send, recv_sem.at[q], to_row, to_col,
                ).start()

    @pl.loop(0, steps - 1)
    def _(q):
        wait_for(held.at[rows_of(q)], recv_sem.at[q])
        convolve(held, mix_ref, flux, q * part, part)

    wait_for(held.at[rows_of(steps - 1)], recv_sem.at[steps - 1])

    wait_for(own_tile, coef_send.at[0])
    wait_for(tiles(near), coef_send.at[1])
    wait_for(tiles(near), coef_send.at[2])
    wait_for(held.at[:, pl.ds(0, near * local)], near_send)

    @pl.when(raw)
    def _():
        wait_for(x.at[:, local : local + GROUP, far_rows], raw_send)
        edge_copy.wait_send()
        wait_for(held.at[:, pl.ds(0, (near + 1) * (local - GROUP))], cross_send)
        wait_for(held.at[:, pl.ds(0, near * GROUP)], relay_send)

    @pl.when(jnp.logical_not(raw))
    def _():
        wait_for(held.at[:, pl.ds(0, (near + 1) * local)], cross_send)


def convolve(held, mix_ref, flux, begin, count):
    total, width = held.shape[1], held.shape[2]
    x = jnp.transpose(held[pl.ds(begin, count)], (0, 2, 1)).reshape(count * width, total)
    high = x.astype(jnp.bfloat16)
    low = (x - high.astype(jnp.float32)).astype(jnp.bfloat16)
    cut = total // 2
    for a, b in ((0, cut), (cut, total)):
        out = jnp.dot(high[:, :b], mix_ref[0, :b, a:b], preferred_element_type=jnp.float32)
        out += jnp.dot(low[:, :b], mix_ref[0, :b, a:b], preferred_element_type=jnp.float32)
        out += jnp.dot(high[:, :b], mix_ref[1, :b, a:b], preferred_element_type=jnp.float32)
        flux[pl.ds(begin, count), :, a:b] = out.reshape(count, width, b - a)


def finish_kernel(part, held, flux, mix_ref, out, last, sem):
    rows = held.shape[0]
    ready = rows - part
    early = pltpu.make_async_copy(flux.at[0:ready], out.at[0:ready], sem.at[0])
    early.start()
    convolve(held.at[ready:rows], mix_ref, last, 0, part)
    late = pltpu.make_async_copy(last, out.at[ready:rows], sem.at[1])
    late.start()
    early.wait()
    late.wait()


def per_device(frames, class_index, surface_mask, effusivity, conductivity):
    rows = lax.axis_size("row")
    cols = lax.axis_size("col")
    local, height, width = frames.shape
    tile_rows, tile_cols = height // rows, width // cols
    total = local * rows * cols
    near = rows // 2 * cols - 1
    fits = (
        rows % 2 == 0 and cols % 2 == 0 and local % (2 * GROUP) == 0 and tile_rows % PAD == 0
        and tile_rows % STEPS == 0 and tile_cols == LANES and total % (2 * LANES) == 0
        and near <= tile_rows and 2 * tile_rows <= total
    )
    if not fits:
        return plain_device(frames, class_index, surface_mask, effusivity, conductivity)
    half_rows, span = height // 2, height // 2 + 2 * PASSES
    vmem = pl.BlockSpec(memory_space=pltpu.VMEM)
    hbm = pl.BlockSpec(memory_space=pltpu.HBM)
    dma = pltpu.SemaphoreType.DMA
    f32 = jnp.float32
    arguments = (frames, class_index, surface_mask, effusivity, conductivity)
    held, flux, mix = pl.pallas_call(
        functools.partial(gather_kernel, rows, cols, tile_rows, tile_cols, local, height, STEPS),
        out_shape=(
            jax.ShapeDtypeStruct((tile_rows, total, LANES), f32),
            jax.ShapeDtypeStruct((tile_rows, tile_cols, total), f32),
            jax.ShapeDtypeStruct((2, total, total), jnp.bfloat16),
        ),
        in_specs=[hbm] * 5,
        out_specs=(vmem, vmem, vmem),
        scratch_shapes=[
            pltpu.VMEM((cols, local + GROUP, height, LANES), f32),
            pltpu.VMEM((cols, 2, height + 2 * PAD, LANES), f32),
            pltpu.VMEM((rows, cols, tile_rows, local, LANES), f32),
            pltpu.VMEM((rows // 2, cols, tile_rows, GROUP, LANES), f32),
            pltpu.VMEM((span, cols, GROUP, LANES), f32),
            pltpu.VMEM((span, cols, GROUP, LANES), f32),
            pltpu.VMEM((PASSES, cols, GROUP, LANES), f32),
            pltpu.VMEM((PASSES, cols, GROUP, LANES), f32),
            pltpu.VMEM((tile_rows, tile_cols), jnp.int32),
            pltpu.VMEM((tile_rows, tile_cols), jnp.int32),
            pltpu.SMEM(effusivity.shape, f32),
            pltpu.SMEM(conductivity.shape, f32),
            dma, dma((4,)), dma((3,)), dma, dma, dma,
            dma, dma, dma, dma,
            dma, dma, dma, dma((STEPS,)),
        ],
        compiler_params=pltpu.CompilerParams(
            collective_id=0, has_side_effects=True, vmem_limit_bytes=VMEM_GATHER
        ),
        name="gather",
    )(*(pltpu.with_memory_space_constraint(a, pltpu.HBM) for a in arguments))
    part = tile_rows // STEPS
    return pl.pallas_call(
        functools.partial(finish_kernel, part),
        out_shape=jax.ShapeDtypeStruct((tile_rows, tile_cols, total), f32),
        in_specs=[vmem, vmem, vmem],
        out_specs=hbm,
        scratch_shapes=[pltpu.VMEM((part, tile_cols, total), f32), dma((2,))],
        compiler_params=pltpu.CompilerParams(vmem_limit_bytes=24 * 2**20),
        name="finish",
    )(held, flux, mix)


def solution(mesh):
    in_specs = (P(("row", "col"), None, None), P("row", "col"), P("row", "col"), P(), P())
    out_specs = P("row", "col", None)
    return jax.shard_map(
        per_device, mesh=mesh, in_specs=in_specs, out_specs=out_specs, check_vma=False
    )
```

```python
import functools
import jax
import jax.numpy as jnp
from jax import lax
from jax.experimental import pallas as pl
from jax.experimental.pallas import tpu as pltpu
from jax.sharding import PartitionSpec as P

PASSES = 3
PAD = 8
GROUP = 8
LANES = 128
STEPS = 8
ROWS = 12
LINES = 16
VMEM_GATHER = 40 * 2**20
MESH = pl.DeviceIdType.MESH

flux_factor = 1.1283791670955126
lateral_rate = 0.24


def extended(block, sides, width):
    for axis, dim in sides:
        count = lax.axis_size(axis)
        forward = [(i, i + 1) for i in range(count - 1)]
        backward = [(target, source) for source, target in forward]
        low = lax.ppermute(
            lax.slice_in_dim(block, block.shape[dim] - width, None, axis=dim), axis, forward
        )
        high = lax.ppermute(lax.slice_in_dim(block, 0, width, axis=dim), axis, backward)
        block = jnp.concatenate([low, block, high], axis=dim)
    return block


def weights(lagged):
    clipped = jnp.maximum(lagged, 0.0)
    return jnp.where(lagged >= 0.0, 1.0 / (jnp.sqrt(clipped) + jnp.sqrt(clipped + 1.0)), 0.0)


def kernel_from(later, earlier):
    lagged = (later[:, None] - earlier[None, :]).astype(jnp.float32)
    return weights(lagged) - weights(lagged - 1.0)


def relax_once(padded, lateral):
    center = padded[1:-1, 1:-1]
    laplace = (
        padded[2:, 1:-1] + padded[:-2, 1:-1] + padded[1:-1, 2:] + padded[1:-1, :-2] - 4.0 * center
    )
    return center + lateral[:, :, None] * laplace


def plain_device(frames, class_index, surface_mask, effusivity, conductivity):
    row_count = lax.axis_size("row")
    col_count = lax.axis_size("col")
    local_frames, height, width = frames.shape
    tile_rows = height // row_count
    tile_cols = width // col_count
    total_frames = local_frames * row_count * col_count
    frame_ids = jnp.arange(total_frames, dtype=jnp.int32)
    contract = (((0,), (1,)), ((), ()))
    kernel = kernel_from(frame_ids, frame_ids)
    blocks = frames.reshape(local_frames, row_count, tile_rows, col_count, tile_cols)
    blocks = blocks.transpose(0, 1, 3, 2, 4).reshape(
        local_frames, row_count * col_count, tile_rows, tile_cols
    )
    convolved = lax.dot_general(
        lax.all_to_all(blocks, ("row", "col"), split_axis=1, concat_axis=0, tiled=True)[:, 0],
        kernel,
        contract,
        precision=lax.Precision.HIGHEST,
    )
    classes = jnp.arange(effusivity.shape[0], dtype=jnp.int32)
    matches = (class_index[:, :, None] == classes[None, None, :]).astype(jnp.float32)
    maskf = surface_mask.astype(jnp.float32)
    gain = flux_factor * jnp.sum(matches * effusivity, axis=-1) * maskf
    lateral = lateral_rate * jnp.sum(matches * conductivity, axis=-1) * maskf
    heat_flux = convolved * gain[:, :, None]
    padded = extended(heat_flux, (("row", 0), ("col", 1)), PASSES)
    lateral_wide = extended(lateral, (("row", 0), ("col", 1)), PASSES - 1)
    for pass_index in range(PASSES):
        margin = PASSES - 1 - pass_index
        offset = PASSES - 1 - margin
        lateral_part = lateral_wide[
            offset : offset + tile_rows + 2 * margin, offset : offset + tile_cols + 2 * margin
        ]
        padded = relax_once(padded, lateral_part)
    return padded


def gather_kernel(
    rows, cols, tile_rows, tile_cols, local, height, steps,
    frames, class_in, mask_in, eff_in, cond_in,
    held, flux, mix_ref,
    x, coef, done, done_far, first, second, edge_out, edge_in,
    class_ref, mask_ref, eff_ref, cond_ref,
    load_sem, small_sem, coef_send, near_recv, pair_recv, far_recv,
    raw_send, raw_recv, edge_send, edge_recv,
    near_send, cross_send, relay_send, recv_sem,
):
    row, col = lax.axis_index("row"), lax.axis_index("col")
    mid = rows // 2
    half = row // mid
    other = 1 - half
    half_rows = height // 2
    total = rows * cols * local
    halo = PASSES
    near = mid * cols - 1
    part = tile_rows // steps
    source = row * cols + col
    mirror, pair = rows - 1 - row, lax.rem(row + mid, rows)
    raw = (row == mid - 1) | (row == mid)

    def wait_for(ref, sem):
        pltpu.make_async_copy(ref, ref, sem).wait()

    def aligned(value, unit):
        return pl.multiple_of(value, unit)

    def remote(src, dst, send, recv, to_row, to_col):
        return pltpu.make_async_remote_copy(
            src_ref=src, dst_ref=dst, send_sem=send, recv_sem=recv,
            device_id=(to_row, to_col), device_id_type=MESH,
        )

    def in_half(i):
        at = lax.rem(row * cols + col - half * (near + 1) + i, near + 1)
        return half * mid + at // cols, lax.rem(at, cols)

    smalls = [
        pltpu.make_async_copy(src, dst, small_sem.at[i])
        for i, (src, dst) in enumerate(
            ((class_in, class_ref), (mask_in, mask_ref), (eff_in, eff_ref), (cond_in, cond_ref))
        )
    ]
    for copy in smalls:
        copy.start()
    for c in range(cols):
        pltpu.make_async_copy(
            frames.at[:, :, c * LANES : (c + 1) * LANES], x.at[c, 0:local], load_sem
        ).start()

    barrier = pltpu.get_barrier_semaphore()

    @pl.when(raw)
    def _():
        pl.semaphore_signal(barrier, inc=1, device_id=(mirror, col), device_id_type=MESH)

    pl.semaphore_signal(barrier, inc=1, device_id=(pair, col), device_id_type=MESH)

    @pl.loop(1, near + 1)
    def _(i):
        pl.semaphore_signal(barrier, inc=1, device_id=in_half(i), device_id_type=MESH)

    for copy in smalls:
        copy.wait()
    classes = class_ref[...]
    maskf = mask_ref[...].astype(jnp.float32)
    eff = jnp.zeros(classes.shape, jnp.float32)
    cond = jnp.zeros(classes.shape, jnp.float32)
    for k in range(eff_ref.shape[0]):
        eff = jnp.where(classes == k, eff_ref[k], eff)
        cond = jnp.where(classes == k, cond_ref[k], cond)

    def tile_of(at_row, at_col):
        return coef.at[at_col, :, pl.ds(aligned(PAD + at_row * tile_rows, PAD), tile_rows)]

    own_rows = pl.ds(aligned(PAD + row * tile_rows, PAD), tile_rows)
    coef[col, 0, own_rows] = lateral_rate * cond * maskf
    coef[col, 1, own_rows] = flux_factor * eff * maskf
    for c in range(cols):
        for k in range(2):
            coef[c, k, 0:PAD] = jnp.zeros((PAD, LANES), jnp.float32)
            coef[c, k, PAD + height : 2 * PAD + height] = jnp.zeros((PAD, LANES), jnp.float32)

    pl.semaphore_wait(barrier, near + 1 + raw.astype(jnp.int32))

    own_tile, pair_tile = tile_of(row, col), tile_of(pair, col)
    remote(own_tile, own_tile, coef_send.at[0], pair_recv, pair, col).start()

    @pl.loop(1, near + 1)
    def _(i):
        to_row, to_col = in_half(i)
        remote(own_tile, own_tile, coef_send.at[1], near_recv, to_row, to_col).start()

    far_rows = pl.ds(aligned(other * half_rows, PAD), half_rows)
    near_rows = pl.ds(aligned(half * half_rows, PAD), half_rows)

    def raw_copy(c):
        return remote(
            frames.at[0:GROUP, far_rows, c * LANES : (c + 1) * LANES],
            x.at[c, local : local + GROUP, far_rows],
            raw_send, raw_recv, mirror, col,
        )

    edge_copy = remote(edge_out, edge_in, edge_send, edge_recv, mirror, col)

    @pl.when(raw)
    def _():
        for c in range(cols):
            raw_copy(c).start()

    wait_for(x.at[:, 0:local], load_sem)
    lines = x.reshape(cols, (local + GROUP) * height, LANES)

    def line(c, group, at):
        return lines[c, pl.ds(group * (GROUP * height) + at, GROUP, stride=height), :]

    @pl.when(raw)
    def _():
        for k in range(halo):
            for c in range(cols):
                edge_out[k, c] = line(c, 0, half_rows - halo * other + k)
        edge_copy.start()

    def fill_mix():
        block = tile_cols

        @pl.loop(0, total // block)
        def _(k):
            shape = (block, total)
            earlier = lax.broadcasted_iota(jnp.int32, shape, 0) + k * block
            later = lax.broadcasted_iota(jnp.int32, shape, 1)
            lagged = (later - earlier).astype(jnp.float32)
            mix = weights(lagged) - weights(lagged - 1.0)
            high = mix.astype(jnp.bfloat16)
            at = pl.ds(aligned(k * block, block), block)
            mix_ref[0, at] = high
            mix_ref[1, at] = (mix - high.astype(jnp.float32)).astype(jnp.bfloat16)

    lane = lax.broadcasted_iota(jnp.int32, (GROUP, LANES), 1)
    leftmost, rightmost = lane == 0, lane == LANES - 1
    nothing = jnp.zeros((GROUP, LANES), jnp.float32)

    def spread(c, which, at):
        return coef[c, which, pl.ds(at, GROUP, stride=0), :]

    def relax(source_ref, side, begin, end, unroll, store):
        base = side * half_rows - halo + PAD

        @pl.loop(begin, end, step=unroll)
        def _(i):
            lines_at = [[source_ref[i + k, c] for c in range(cols)] for k in range(-1, unroll + 1)]
            for k in range(unroll):
                above, center, below = lines_at[k : k + 3]
                ahead = [pltpu.roll(v, 1, 1) for v in center]
                behind = [pltpu.roll(v, LANES - 1, 1) for v in center]
                for c in range(cols):
                    left = jnp.where(leftmost, ahead[c - 1] if c else nothing, ahead[c])
                    right = jnp.where(rightmost, behind[c + 1] if c + 1 < cols else nothing, behind[c])
                    laplace = below[c] + above[c] + right + left - 4.0 * center[c]
                    store(i + k, c, center[c] + spread(c, 0, base + i + k) * laplace)

    def keep(ref):
        def store(i, c, value):
            ref[i, c] = value
        return store

    def sweep(side, group, edge, store_last):
        span = half_rows + 2 * halo
        for k in range(halo):
            at = half_rows - halo * side + k
            for c in range(cols):
                first[(half_rows + halo) * side + k, c] = nothing
                first[(half_rows + halo) * (1 - side) + k, c] = spread(c, 1, at + PAD) * edge(k, c, at)
        for c in range(cols):
            second[0, c] = nothing
            second[span - 1, c] = nothing

        @pl.loop(0, half_rows, step=LINES)
        def _(j):
            for k in range(LINES):
                at = half_rows * side + j + k
                for c in range(cols):
                    first[halo + j + k, c] = spread(c, 1, at + PAD) * line(c, group, at)

        relax(first, side, 1, span - 1, ROWS, keep(second))
        relax(second, side, 1, span - 1, ROWS, keep(first))
        relax(first, side, halo, span - halo, LINES, store_last)

    def sweep_own(side, group):
        def store(i, c, value):
            j = i - halo
            at = pl.ds(aligned(group * GROUP, GROUP), GROUP)
            done[side * mid + j // tile_rows, c, lax.rem(j, tile_rows), at, :] = value

        sweep(side, group, lambda k, c, at: line(c, group, at), store)

    def sweep_raw():
        def store(i, c, value):
            j = i - halo
            done_far[j // tile_rows, c, lax.rem(j, tile_rows), :, :] = value

        sweep(half, local // GROUP, lambda k, c, at: edge_in[k, c], store)

    groups = local // GROUP

    def rows_of(q):
        return pl.ds(q * part, part)

    def slots(at, count):
        return pl.ds(aligned(at, GROUP), count)

    fill_mix()

    wait_for(pair_tile, pair_recv)

    @pl.loop(1, near + 1)
    def _(i):
        to_row, to_col = in_half(i)
        remote(pair_tile, pair_tile, coef_send.at[2], far_recv, to_row, to_col).start()

    def tiles(count):
        return held.at[pl.ds(0, count), pl.ds(0, 2 * tile_rows)]

    wait_for(tiles(near), near_recv)
    wait_for(tiles(near), far_recv)

    @pl.loop(0, groups)
    def _(g):
        sweep_own(half, g)

    own_slots = slots(source * local, local)

    def near_copy(q, i):
        to_row, to_col = in_half(i)
        return remote(
            done.at[to_row, to_col, rows_of(q)], held.at[rows_of(q), own_slots],
            near_send, recv_sem.at[q], to_row, to_col,
        )

    @pl.loop(0, steps)
    def _(q):
        pltpu.make_async_copy(
            done.at[row, col, rows_of(q)], held.at[rows_of(q), own_slots], recv_sem.at[q]
        ).start()

        @pl.loop(1, near + 1)
        def _(i):
            near_copy(q, i).start()

    @pl.loop(raw.astype(jnp.int32), groups)
    def _(g):
        sweep_own(other, g)

    def across(i):
        at = lax.rem(row * cols + col - half * (near + 1) + i, near + 1)
        return other * mid + at // cols, lax.rem(at, cols)

    def start_cross(skip):
        count = local - skip

        @pl.loop(0, steps)
        def _(q):
            @pl.loop(0, near + 1)
            def _(i):
                to_row, to_col = across(i)
                remote(
                    done.at[to_row, to_col, rows_of(q), pl.ds(skip, count)],
                    held.at[rows_of(q), slots(source * local + skip, count)],
                    cross_send, recv_sem.at[q], to_row, to_col,
                ).start()

    @pl.when(raw)
    def _():
        start_cross(GROUP)

    @pl.when(jnp.logical_not(raw))
    def _():
        start_cross(0)

    @pl.when(raw)
    def _():
        wait_for(x.at[:, local : local + GROUP, near_rows], raw_recv)
        edge_copy.wait_recv()
        sweep_raw()
        there = slots((mirror * cols + col) * local, GROUP)

        @pl.loop(0, steps)
        def _(q):
            pltpu.make_async_copy(
                done_far.at[row - half * mid, col, rows_of(q)], held.at[rows_of(q), there],
                recv_sem.at[q],
            ).start()

            @pl.loop(1, near + 1)
            def _(i):
                to_row, to_col = in_half(i)
                remote(
                    done_far.at[to_row - half * mid, to_col, rows_of(q)],
                    held.at[rows_of(q), there],
                    relay_send, recv_sem.at[q], to_row, to_col,
                ).start()

    @pl.loop(0, steps - 1)
    def _(q):
        wait_for(held.at[rows_of(q)], recv_sem.at[q])
        convolve(held, mix_ref, flux, q * part, part)

    wait_for(held.at[rows_of(steps - 1)], recv_sem.at[steps - 1])

    wait_for(own_tile, coef_send.at[0])
    wait_for(tiles(near), coef_send.at[1])
    wait_for(tiles(near), coef_send.at[2])
    wait_for(held.at[:, pl.ds(0, near * local)], near_send)

    @pl.when(raw)
    def _():
        wait_for(x.at[:, local : local + GROUP, far_rows], raw_send)
        edge_copy.wait_send()
        wait_for(held.at[:, pl.ds(0, (near + 1) * (local - GROUP))], cross_send)
        wait_for(held.at[:, pl.ds(0, near * GROUP)], relay_send)

    @pl.when(jnp.logical_not(raw))
    def _():
        wait_for(held.at[:, pl.ds(0, (near + 1) * local)], cross_send)


def convolve(held, mix_ref, flux, begin, count):
    total, width = held.shape[1], held.shape[2]
    x = jnp.transpose(held[pl.ds(begin, count)], (0, 2, 1)).reshape(count * width, total)
    high = x.astype(jnp.bfloat16)
    low = (x - high.astype(jnp.float32)).astype(jnp.bfloat16)
    cut = total // 2
    for a, b in ((0, cut), (cut, total)):
        out = jnp.dot(high[:, :b], mix_ref[0, :b, a:b], preferred_element_type=jnp.float32)
        out += jnp.dot(low[:, :b], mix_ref[0, :b, a:b], preferred_element_type=jnp.float32)
        out += jnp.dot(high[:, :b], mix_ref[1, :b, a:b], preferred_element_type=jnp.float32)
        flux[pl.ds(begin, count), :, a:b] = out.reshape(count, width, b - a)


def finish_kernel(part, held, flux, mix_ref, out, last, sem):
    rows = held.shape[0]
    ready = rows - part
    early = pltpu.make_async_copy(flux.at[0:ready], out.at[0:ready], sem.at[0])
    early.start()
    convolve(held.at[ready:rows], mix_ref, last, 0, part)
    late = pltpu.make_async_copy(last, out.at[ready:rows], sem.at[1])
    late.start()
    early.wait()
    late.wait()


def per_device(frames, class_index, surface_mask, effusivity, conductivity):
    rows = lax.axis_size("row")
    cols = lax.axis_size("col")
    local, height, width = frames.shape
    tile_rows, tile_cols = height // rows, width // cols
    total = local * rows * cols
    near = rows // 2 * cols - 1
    fits = (
        rows % 2 == 0 and cols % 2 == 0 and local % (2 * GROUP) == 0 and tile_rows % PAD == 0
        and tile_rows % STEPS == 0 and tile_cols == LANES and total % (2 * LANES) == 0
        and near <= tile_rows and 2 * tile_rows <= total
        and height // 2 % LINES == 0 and (height // 2 + 2 * PASSES - 2) % ROWS == 0
    )
    if not fits:
        return plain_device(frames, class_index, surface_mask, effusivity, conductivity)
    half_rows, span = height // 2, height // 2 + 2 * PASSES
    vmem = pl.BlockSpec(memory_space=pltpu.VMEM)
    hbm = pl.BlockSpec(memory_space=pltpu.HBM)
    dma = pltpu.SemaphoreType.DMA
    f32 = jnp.float32
    arguments = (frames, class_index, surface_mask, effusivity, conductivity)
    held, flux, mix = pl.pallas_call(
        functools.partial(gather_kernel, rows, cols, tile_rows, tile_cols, local, height, STEPS),
        out_shape=(
            jax.ShapeDtypeStruct((tile_rows, total, LANES), f32),
            jax.ShapeDtypeStruct((tile_rows, tile_cols, total), f32),
            jax.ShapeDtypeStruct((2, total, total), jnp.bfloat16),
        ),
        in_specs=[hbm] * 5,
        out_specs=(vmem, vmem, vmem),
        scratch_shapes=[
            pltpu.VMEM((cols, local + GROUP, height, LANES), f32),
            pltpu.VMEM((cols, 2, height + 2 * PAD, LANES), f32),
            pltpu.VMEM((rows, cols, tile_rows, local, LANES), f32),
            pltpu.VMEM((rows // 2, cols, tile_rows, GROUP, LANES), f32),
            pltpu.VMEM((span, cols, GROUP, LANES), f32),
            pltpu.VMEM((span, cols, GROUP, LANES), f32),
            pltpu.VMEM((PASSES, cols, GROUP, LANES), f32),
            pltpu.VMEM((PASSES, cols, GROUP, LANES), f32),
            pltpu.VMEM((tile_rows, tile_cols), jnp.int32),
            pltpu.VMEM((tile_rows, tile_cols), jnp.int32),
            pltpu.SMEM(effusivity.shape, f32),
            pltpu.SMEM(conductivity.shape, f32),
            dma, dma((4,)), dma((3,)), dma, dma, dma,
            dma, dma, dma, dma,
            dma, dma, dma, dma((STEPS,)),
        ],
        compiler_params=pltpu.CompilerParams(
            collective_id=0, has_side_effects=True, vmem_limit_bytes=VMEM_GATHER
        ),
        name="gather",
    )(*(pltpu.with_memory_space_constraint(a, pltpu.HBM) for a in arguments))
    part = tile_rows // STEPS
    return pl.pallas_call(
        functools.partial(finish_kernel, part),
        out_shape=jax.ShapeDtypeStruct((tile_rows, tile_cols, total), f32),
        in_specs=[vmem, vmem, vmem],
        out_specs=hbm,
        scratch_shapes=[pltpu.VMEM((part, tile_cols, total), f32), dma((2,))],
        compiler_params=pltpu.CompilerParams(vmem_limit_bytes=24 * 2**20),
        name="finish",
    )(held, flux, mix)


def solution(mesh):
    in_specs = (P(("row", "col"), None, None), P("row", "col"), P("row", "col"), P(), P())
    out_specs = P("row", "col", None)
    return jax.shard_map(
        per_device, mesh=mesh, in_specs=in_specs, out_specs=out_specs, check_vma=False
    )
```

```python
import functools
import jax
import jax.numpy as jnp
from jax import lax
from jax.experimental import pallas as pl
from jax.experimental.pallas import tpu as pltpu
from jax.sharding import PartitionSpec as P

PASSES = 3
PAD = 8
GROUP = 8
LANES = 128
STEPS = 4
ROWS = 12
LINES = 16
VMEM_GATHER = 40 * 2**20
MESH = pl.DeviceIdType.MESH

flux_factor = 1.1283791670955126
lateral_rate = 0.24


def extended(block, sides, width):
    for axis, dim in sides:
        count = lax.axis_size(axis)
        forward = [(i, i + 1) for i in range(count - 1)]
        backward = [(target, source) for source, target in forward]
        low = lax.ppermute(
            lax.slice_in_dim(block, block.shape[dim] - width, None, axis=dim), axis, forward
        )
        high = lax.ppermute(lax.slice_in_dim(block, 0, width, axis=dim), axis, backward)
        block = jnp.concatenate([low, block, high], axis=dim)
    return block


def weights(lagged):
    clipped = jnp.maximum(lagged, 0.0)
    return jnp.where(lagged >= 0.0, 1.0 / (jnp.sqrt(clipped) + jnp.sqrt(clipped + 1.0)), 0.0)


def kernel_from(later, earlier):
    lagged = (later[:, None] - earlier[None, :]).astype(jnp.float32)
    return weights(lagged) - weights(lagged - 1.0)


def relax_once(padded, lateral):
    center = padded[1:-1, 1:-1]
    laplace = (
        padded[2:, 1:-1] + padded[:-2, 1:-1] + padded[1:-1, 2:] + padded[1:-1, :-2] - 4.0 * center
    )
    return center + lateral[:, :, None] * laplace


def plain_device(frames, class_index, surface_mask, effusivity, conductivity):
    row_count = lax.axis_size("row")
    col_count = lax.axis_size("col")
    local_frames, height, width = frames.shape
    tile_rows = height // row_count
    tile_cols = width // col_count
    total_frames = local_frames * row_count * col_count
    frame_ids = jnp.arange(total_frames, dtype=jnp.int32)
    contract = (((0,), (1,)), ((), ()))
    kernel = kernel_from(frame_ids, frame_ids)
    blocks = frames.reshape(local_frames, row_count, tile_rows, col_count, tile_cols)
    blocks = blocks.transpose(0, 1, 3, 2, 4).reshape(
        local_frames, row_count * col_count, tile_rows, tile_cols
    )
    convolved = lax.dot_general(
        lax.all_to_all(blocks, ("row", "col"), split_axis=1, concat_axis=0, tiled=True)[:, 0],
        kernel,
        contract,
        precision=lax.Precision.HIGHEST,
    )
    classes = jnp.arange(effusivity.shape[0], dtype=jnp.int32)
    matches = (class_index[:, :, None] == classes[None, None, :]).astype(jnp.float32)
    maskf = surface_mask.astype(jnp.float32)
    gain = flux_factor * jnp.sum(matches * effusivity, axis=-1) * maskf
    lateral = lateral_rate * jnp.sum(matches * conductivity, axis=-1) * maskf
    heat_flux = convolved * gain[:, :, None]
    padded = extended(heat_flux, (("row", 0), ("col", 1)), PASSES)
    lateral_wide = extended(lateral, (("row", 0), ("col", 1)), PASSES - 1)
    for pass_index in range(PASSES):
        margin = PASSES - 1 - pass_index
        offset = PASSES - 1 - margin
        lateral_part = lateral_wide[
            offset : offset + tile_rows + 2 * margin, offset : offset + tile_cols + 2 * margin
        ]
        padded = relax_once(padded, lateral_part)
    return padded


def gather_kernel(
    rows, cols, tile_rows, tile_cols, local, height, steps,
    frames, class_in, mask_in, eff_in, cond_in,
    held, flux, mix_ref,
    x, coef, done, done_far, first, second, edge_out, edge_in,
    class_ref, mask_ref, eff_ref, cond_ref,
    load_sem, small_sem, coef_send, near_recv, pair_recv, far_recv,
    raw_send, raw_recv, edge_send, edge_recv,
    near_send, cross_send, relay_send, recv_sem,
):
    row, col = lax.axis_index("row"), lax.axis_index("col")
    mid = rows // 2
    half = row // mid
    other = 1 - half
    half_rows = height // 2
    total = rows * cols * local
    halo = PASSES
    near = mid * cols - 1
    part = tile_rows // steps
    source = row * cols + col
    mirror, pair = rows - 1 - row, lax.rem(row + mid, rows)
    inner = (row == mid - 1) | (row == mid)
    raw = inner & (lax.rem(col, 2) == 0)

    def wait_for(ref, sem):
        pltpu.make_async_copy(ref, ref, sem).wait()

    def aligned(value, unit):
        return pl.multiple_of(value, unit)

    def remote(src, dst, send, recv, to_row, to_col):
        return pltpu.make_async_remote_copy(
            src_ref=src, dst_ref=dst, send_sem=send, recv_sem=recv,
            device_id=(to_row, to_col), device_id_type=MESH,
        )

    def in_half(i):
        return half * mid + lax.rem(row + i // cols, mid), lax.rem(col + i, cols)

    smalls = [
        pltpu.make_async_copy(src, dst, small_sem.at[i])
        for i, (src, dst) in enumerate(
            ((class_in, class_ref), (mask_in, mask_ref), (eff_in, eff_ref), (cond_in, cond_ref))
        )
    ]
    for copy in smalls:
        copy.start()
    for c in range(cols):
        pltpu.make_async_copy(
            frames.at[:, :, c * LANES : (c + 1) * LANES], x.at[c, 0:local], load_sem
        ).start()

    barrier = pltpu.get_barrier_semaphore()

    @pl.when(raw)
    def _():
        pl.semaphore_signal(barrier, inc=1, device_id=(mirror, col), device_id_type=MESH)

    pl.semaphore_signal(barrier, inc=1, device_id=(pair, col), device_id_type=MESH)

    @pl.loop(1, near + 1)
    def _(i):
        pl.semaphore_signal(barrier, inc=1, device_id=in_half(i), device_id_type=MESH)

    for copy in smalls:
        copy.wait()
    classes = class_ref[...]
    maskf = mask_ref[...].astype(jnp.float32)
    eff = jnp.zeros(classes.shape, jnp.float32)
    cond = jnp.zeros(classes.shape, jnp.float32)
    for k in range(eff_ref.shape[0]):
        eff = jnp.where(classes == k, eff_ref[k], eff)
        cond = jnp.where(classes == k, cond_ref[k], cond)

    def tile_of(at_row, at_col):
        return coef.at[at_col, :, pl.ds(aligned(PAD + at_row * tile_rows, PAD), tile_rows)]

    own_rows = pl.ds(aligned(PAD + row * tile_rows, PAD), tile_rows)
    coef[col, 0, own_rows] = lateral_rate * cond * maskf
    coef[col, 1, own_rows] = flux_factor * eff * maskf
    for c in range(cols):
        for k in range(2):
            coef[c, k, 0:PAD] = jnp.zeros((PAD, LANES), jnp.float32)
            coef[c, k, PAD + height : 2 * PAD + height] = jnp.zeros((PAD, LANES), jnp.float32)

    pl.semaphore_wait(barrier, near + 1 + raw.astype(jnp.int32))

    own_tile, pair_tile = tile_of(row, col), tile_of(pair, col)
    remote(own_tile, own_tile, coef_send.at[0], pair_recv, pair, col).start()

    @pl.loop(1, near + 1)
    def _(i):
        to_row, to_col = in_half(i)
        remote(own_tile, own_tile, coef_send.at[1], near_recv, to_row, to_col).start()

    far_rows = pl.ds(aligned(other * half_rows, PAD), half_rows)
    near_rows = pl.ds(aligned(half * half_rows, PAD), half_rows)

    def raw_copy(c):
        return remote(
            frames.at[0:GROUP, far_rows, c * LANES : (c + 1) * LANES],
            x.at[c, local : local + GROUP, far_rows],
            raw_send, raw_recv, mirror, col,
        )

    edge_copy = remote(edge_out, edge_in, edge_send, edge_recv, mirror, col)

    @pl.when(raw)
    def _():
        for c in range(cols):
            raw_copy(c).start()

    wait_for(x.at[:, 0:local], load_sem)
    lines = x.reshape(cols, (local + GROUP) * height, LANES)

    def line(c, group, at):
        return lines[c, pl.ds(group * (GROUP * height) + at, GROUP, stride=height), :]

    @pl.when(raw)
    def _():
        for k in range(halo):
            for c in range(cols):
                edge_out[k, c] = line(c, 0, half_rows - halo * other + k)
        edge_copy.start()

    def fill_mix():
        block = tile_cols

        @pl.loop(0, total // block)
        def _(k):
            shape = (block, total)
            earlier = lax.broadcasted_iota(jnp.int32, shape, 0) + k * block
            later = lax.broadcasted_iota(jnp.int32, shape, 1)
            lagged = (later - earlier).astype(jnp.float32)
            mix = weights(lagged) - weights(lagged - 1.0)
            high = mix.astype(jnp.bfloat16)
            at = pl.ds(aligned(k * block, block), block)
            mix_ref[0, at] = high
            mix_ref[1, at] = (mix - high.astype(jnp.float32)).astype(jnp.bfloat16)

    lane = lax.broadcasted_iota(jnp.int32, (GROUP, LANES), 1)
    leftmost, rightmost = lane == 0, lane == LANES - 1
    nothing = jnp.zeros((GROUP, LANES), jnp.float32)

    def spread(c, which, at):
        return coef[c, which, pl.ds(at, GROUP, stride=0), :]

    def relax(source_ref, side, begin, end, unroll, store):
        base = side * half_rows - halo + PAD

        @pl.loop(begin, end, step=unroll)
        def _(i):
            lines_at = [[source_ref[i + k, c] for c in range(cols)] for k in range(-1, unroll + 1)]
            for k in range(unroll):
                above, center, below = lines_at[k : k + 3]
                ahead = [pltpu.roll(v, 1, 1) for v in center]
                behind = [pltpu.roll(v, LANES - 1, 1) for v in center]
                for c in range(cols):
                    left = jnp.where(leftmost, ahead[c - 1] if c else nothing, ahead[c])
                    right = jnp.where(rightmost, behind[c + 1] if c + 1 < cols else nothing, behind[c])
                    laplace = below[c] + above[c] + right + left - 4.0 * center[c]
                    store(i + k, c, center[c] + spread(c, 0, base + i + k) * laplace)

    def keep(ref):
        def store(i, c, value):
            ref[i, c] = value
        return store

    def sweep(side, group, edge, store_last):
        span = half_rows + 2 * halo
        for k in range(halo):
            at = half_rows - halo * side + k
            for c in range(cols):
                first[(half_rows + halo) * side + k, c] = nothing
                first[(half_rows + halo) * (1 - side) + k, c] = spread(c, 1, at + PAD) * edge(k, c, at)
        for c in range(cols):
            second[0, c] = nothing
            second[span - 1, c] = nothing

        @pl.loop(0, half_rows, step=LINES)
        def _(j):
            for k in range(LINES):
                at = half_rows * side + j + k
                for c in range(cols):
                    first[halo + j + k, c] = spread(c, 1, at + PAD) * line(c, group, at)

        relax(first, side, 1, span - 1, ROWS, keep(second))
        relax(second, side, 1, span - 1, ROWS, keep(first))
        relax(first, side, halo, span - halo, LINES, store_last)

    def sweep_own(side, group):
        def store(i, c, value):
            j = i - halo
            at = pl.ds(aligned(group * GROUP, GROUP), GROUP)
            done[side * mid + j // tile_rows, c, lax.rem(j, tile_rows), at, :] = value

        sweep(side, group, lambda k, c, at: line(c, group, at), store)

    def sweep_raw():
        def store(i, c, value):
            j = i - halo
            done_far[j // tile_rows, c, lax.rem(j, tile_rows), :, :] = value

        sweep(half, local // GROUP, lambda k, c, at: edge_in[k, c], store)

    groups = local // GROUP

    def rows_of(q):
        return pl.ds(q * part, part)

    def slots(at, count):
        return pl.ds(aligned(at, GROUP), count)

    fill_mix()

    wait_for(pair_tile, pair_recv)

    @pl.loop(1, near + 1)
    def _(i):
        to_row, to_col = in_half(i)
        remote(pair_tile, pair_tile, coef_send.at[2], far_recv, to_row, to_col).start()

    def tiles(count):
        return held.at[pl.ds(0, count), pl.ds(0, 2 * tile_rows)]

    wait_for(tiles(near), near_recv)
    wait_for(tiles(near), far_recv)

    own_slots = slots(source * local, local)

    def across(i):
        return other * mid + lax.rem(row + i // cols, mid), lax.rem(col + i, cols)

    def send_near(q):
        pltpu.make_async_copy(
            done.at[row, col, rows_of(q)], held.at[rows_of(q), own_slots], recv_sem.at[q]
        ).start()

        @pl.loop(1, near + 1)
        def _(i):
            to_row, to_col = in_half(i)
            remote(
                done.at[to_row, to_col, rows_of(q)], held.at[rows_of(q), own_slots],
                near_send, recv_sem.at[q], to_row, to_col,
            ).start()

    def send_cross(q, skip):
        count = local - skip

        @pl.loop(0, near + 1)
        def _(i):
            to_row, to_col = across(i)
            remote(
                done.at[to_row, to_col, rows_of(q), pl.ds(skip, count)],
                held.at[rows_of(q), slots(source * local + skip, count)],
                cross_send, recv_sem.at[q], to_row, to_col,
            ).start()

    @pl.loop(raw.astype(jnp.int32), groups)
    def _(g):
        sweep_own(other, g)

    @pl.when(raw)
    def _():
        @pl.loop(0, steps)
        def _(q):
            send_cross(q, GROUP)

    @pl.when(inner & jnp.logical_not(raw))
    def _():
        @pl.loop(0, steps)
        def _(q):
            send_cross(q, 0)

    @pl.loop(0, groups)
    def _(g):
        sweep_own(half, g)

    @pl.loop(0, steps)
    def _(q):
        @pl.when(jnp.logical_not(inner))
        def _():
            send_cross(q, 0)

        send_near(q)

    @pl.when(raw)
    def _():
        wait_for(x.at[:, local : local + GROUP, near_rows], raw_recv)
        edge_copy.wait_recv()
        sweep_raw()
        there = slots((mirror * cols + col) * local, GROUP)

        @pl.loop(0, steps)
        def _(q):
            pltpu.make_async_copy(
                done_far.at[row - half * mid, col, rows_of(q)], held.at[rows_of(q), there],
                recv_sem.at[q],
            ).start()

            @pl.loop(1, near + 1)
            def _(i):
                to_row, to_col = in_half(i)
                remote(
                    done_far.at[to_row - half * mid, to_col, rows_of(q)],
                    held.at[rows_of(q), there],
                    relay_send, recv_sem.at[q], to_row, to_col,
                ).start()

    @pl.loop(0, steps - 1)
    def _(q):
        wait_for(held.at[rows_of(q)], recv_sem.at[q])
        convolve(held, mix_ref, flux, q * part, part)

    wait_for(held.at[rows_of(steps - 1)], recv_sem.at[steps - 1])

    wait_for(own_tile, coef_send.at[0])
    wait_for(tiles(near), coef_send.at[1])
    wait_for(tiles(near), coef_send.at[2])
    wait_for(held.at[:, pl.ds(0, near * local)], near_send)

    @pl.when(raw)
    def _():
        wait_for(x.at[:, local : local + GROUP, far_rows], raw_send)
        edge_copy.wait_send()
        wait_for(held.at[:, pl.ds(0, (near + 1) * (local - GROUP))], cross_send)
        wait_for(held.at[:, pl.ds(0, near * GROUP)], relay_send)

    @pl.when(jnp.logical_not(raw))
    def _():
        wait_for(held.at[:, pl.ds(0, (near + 1) * local)], cross_send)


def convolve(held, mix_ref, flux, begin, count):
    total, width = held.shape[1], held.shape[2]
    x = jnp.transpose(held[pl.ds(begin, count)], (0, 2, 1)).reshape(count * width, total)
    high = x.astype(jnp.bfloat16)
    low = (x - high.astype(jnp.float32)).astype(jnp.bfloat16)
    cut = total // 2
    for a, b in ((0, cut), (cut, total)):
        out = jnp.dot(high[:, :b], mix_ref[0, :b, a:b], preferred_element_type=jnp.float32)
        out += jnp.dot(low[:, :b], mix_ref[0, :b, a:b], preferred_element_type=jnp.float32)
        out += jnp.dot(high[:, :b], mix_ref[1, :b, a:b], preferred_element_type=jnp.float32)
        flux[pl.ds(begin, count), :, a:b] = out.reshape(count, width, b - a)


def finish_kernel(part, held, flux, mix_ref, out, last, sem):
    rows = held.shape[0]
    ready = rows - part
    early = pltpu.make_async_copy(flux.at[0:ready], out.at[0:ready], sem.at[0])
    early.start()
    convolve(held.at[ready:rows], mix_ref, last, 0, part)
    late = pltpu.make_async_copy(last, out.at[ready:rows], sem.at[1])
    late.start()
    early.wait()
    late.wait()


def per_device(frames, class_index, surface_mask, effusivity, conductivity):
    rows = lax.axis_size("row")
    cols = lax.axis_size("col")
    local, height, width = frames.shape
    tile_rows, tile_cols = height // rows, width // cols
    total = local * rows * cols
    near = rows // 2 * cols - 1
    fits = (
        rows % 2 == 0 and cols % 2 == 0 and local % (2 * GROUP) == 0 and tile_rows % PAD == 0
        and tile_rows % STEPS == 0 and tile_cols == LANES and total % (2 * LANES) == 0
        and near <= tile_rows and 2 * tile_rows <= total
        and height // 2 % LINES == 0 and (height // 2 + 2 * PASSES - 2) % ROWS == 0
    )
    if not fits:
        return plain_device(frames, class_index, surface_mask, effusivity, conductivity)
    half_rows, span = height // 2, height // 2 + 2 * PASSES
    vmem = pl.BlockSpec(memory_space=pltpu.VMEM)
    hbm = pl.BlockSpec(memory_space=pltpu.HBM)
    dma = pltpu.SemaphoreType.DMA
    f32 = jnp.float32
    arguments = (frames, class_index, surface_mask, effusivity, conductivity)
    held, flux, mix = pl.pallas_call(
        functools.partial(gather_kernel, rows, cols, tile_rows, tile_cols, local, height, STEPS),
        out_shape=(
            jax.ShapeDtypeStruct((tile_rows, total, LANES), f32),
            jax.ShapeDtypeStruct((tile_rows, tile_cols, total), f32),
            jax.ShapeDtypeStruct((2, total, total), jnp.bfloat16),
        ),
        in_specs=[hbm] * 5,
        out_specs=(vmem, vmem, vmem),
        scratch_shapes=[
            pltpu.VMEM((cols, local + GROUP, height, LANES), f32),
            pltpu.VMEM((cols, 2, height + 2 * PAD, LANES), f32),
            pltpu.VMEM((rows, cols, tile_rows, local, LANES), f32),
            pltpu.VMEM((rows // 2, cols, tile_rows, GROUP, LANES), f32),
            pltpu.VMEM((span, cols, GROUP, LANES), f32),
            pltpu.VMEM((span, cols, GROUP, LANES), f32),
            pltpu.VMEM((PASSES, cols, GROUP, LANES), f32),
            pltpu.VMEM((PASSES, cols, GROUP, LANES), f32),
            pltpu.VMEM((tile_rows, tile_cols), jnp.int32),
            pltpu.VMEM((tile_rows, tile_cols), jnp.int32),
            pltpu.SMEM(effusivity.shape, f32),
            pltpu.SMEM(conductivity.shape, f32),
            dma, dma((4,)), dma((3,)), dma, dma, dma,
            dma, dma, dma, dma,
            dma, dma, dma, dma((STEPS,)),
        ],
        compiler_params=pltpu.CompilerParams(
            collective_id=0, has_side_effects=True, vmem_limit_bytes=VMEM_GATHER
        ),
        name="gather",
    )(*(pltpu.with_memory_space_constraint(a, pltpu.HBM) for a in arguments))
    part = tile_rows // STEPS
    return pl.pallas_call(
        functools.partial(finish_kernel, part),
        out_shape=jax.ShapeDtypeStruct((tile_rows, tile_cols, total), f32),
        in_specs=[vmem, vmem, vmem],
        out_specs=hbm,
        scratch_shapes=[pltpu.VMEM((part, tile_cols, total), f32), dma((2,))],
        compiler_params=pltpu.CompilerParams(vmem_limit_bytes=24 * 2**20),
        name="finish",
    )(held, flux, mix)


def solution(mesh):
    in_specs = (P(("row", "col"), None, None), P("row", "col"), P("row", "col"), P(), P())
    out_specs = P("row", "col", None)
    return jax.shard_map(
        per_device, mesh=mesh, in_specs=in_specs, out_specs=out_specs, check_vma=False
    )
```

```python
import functools
import jax
import jax.numpy as jnp
from jax import lax
from jax.experimental import pallas as pl
from jax.experimental.pallas import tpu as pltpu
from jax.sharding import PartitionSpec as P

PASSES = 3
PAD = 8
GROUP = 8
LANES = 128
STEPS = 4
ROWS = 12
LINES = 16
EARLY = 1
VMEM_GATHER = 40 * 2**20
MESH = pl.DeviceIdType.MESH

flux_factor = 1.1283791670955126
lateral_rate = 0.24


def extended(block, sides, width):
    for axis, dim in sides:
        count = lax.axis_size(axis)
        forward = [(i, i + 1) for i in range(count - 1)]
        backward = [(target, source) for source, target in forward]
        low = lax.ppermute(
            lax.slice_in_dim(block, block.shape[dim] - width, None, axis=dim), axis, forward
        )
        high = lax.ppermute(lax.slice_in_dim(block, 0, width, axis=dim), axis, backward)
        block = jnp.concatenate([low, block, high], axis=dim)
    return block


def weights(lagged):
    clipped = jnp.maximum(lagged, 0.0)
    return jnp.where(lagged >= 0.0, 1.0 / (jnp.sqrt(clipped) + jnp.sqrt(clipped + 1.0)), 0.0)


def kernel_from(later, earlier):
    lagged = (later[:, None] - earlier[None, :]).astype(jnp.float32)
    return weights(lagged) - weights(lagged - 1.0)


def relax_once(padded, lateral):
    center = padded[1:-1, 1:-1]
    laplace = (
        padded[2:, 1:-1] + padded[:-2, 1:-1] + padded[1:-1, 2:] + padded[1:-1, :-2] - 4.0 * center
    )
    return center + lateral[:, :, None] * laplace


def plain_device(frames, class_index, surface_mask, effusivity, conductivity):
    row_count = lax.axis_size("row")
    col_count = lax.axis_size("col")
    local_frames, height, width = frames.shape
    tile_rows = height // row_count
    tile_cols = width // col_count
    total_frames = local_frames * row_count * col_count
    frame_ids = jnp.arange(total_frames, dtype=jnp.int32)
    contract = (((0,), (1,)), ((), ()))
    kernel = kernel_from(frame_ids, frame_ids)
    blocks = frames.reshape(local_frames, row_count, tile_rows, col_count, tile_cols)
    blocks = blocks.transpose(0, 1, 3, 2, 4).reshape(
        local_frames, row_count * col_count, tile_rows, tile_cols
    )
    convolved = lax.dot_general(
        lax.all_to_all(blocks, ("row", "col"), split_axis=1, concat_axis=0, tiled=True)[:, 0],
        kernel,
        contract,
        precision=lax.Precision.HIGHEST,
    )
    classes = jnp.arange(effusivity.shape[0], dtype=jnp.int32)
    matches = (class_index[:, :, None] == classes[None, None, :]).astype(jnp.float32)
    maskf = surface_mask.astype(jnp.float32)
    gain = flux_factor * jnp.sum(matches * effusivity, axis=-1) * maskf
    lateral = lateral_rate * jnp.sum(matches * conductivity, axis=-1) * maskf
    heat_flux = convolved * gain[:, :, None]
    padded = extended(heat_flux, (("row", 0), ("col", 1)), PASSES)
    lateral_wide = extended(lateral, (("row", 0), ("col", 1)), PASSES - 1)
    for pass_index in range(PASSES):
        margin = PASSES - 1 - pass_index
        offset = PASSES - 1 - margin
        lateral_part = lateral_wide[
            offset : offset + tile_rows + 2 * margin, offset : offset + tile_cols + 2 * margin
        ]
        padded = relax_once(padded, lateral_part)
    return padded


def gather_kernel(
    rows, cols, tile_rows, tile_cols, local, height, steps,
    frames, class_in, mask_in, eff_in, cond_in,
    held, flux, mix_ref,
    x, coef, done, done_far, first, second, edge_out, edge_in,
    class_ref, mask_ref, eff_ref, cond_ref,
    load_sem, small_sem, coef_send, near_recv, pair_recv, far_recv,
    raw_send, raw_recv, edge_send, edge_recv,
    near_send, cross_send, relay_send, recv_sem, ready,
):
    row, col = lax.axis_index("row"), lax.axis_index("col")
    mid = rows // 2
    half = row // mid
    other = 1 - half
    half_rows = height // 2
    total = rows * cols * local
    halo = PASSES
    near = mid * cols - 1
    part = tile_rows // steps
    source = row * cols + col
    mirror, pair = rows - 1 - row, lax.rem(row + mid, rows)
    inner = (row == mid - 1) | (row == mid)
    raw = inner & (lax.rem(col, 2) == 0)

    def wait_for(ref, sem):
        pltpu.make_async_copy(ref, ref, sem).wait()

    def aligned(value, unit):
        return pl.multiple_of(value, unit)

    def remote(src, dst, send, recv, to_row, to_col):
        return pltpu.make_async_remote_copy(
            src_ref=src, dst_ref=dst, send_sem=send, recv_sem=recv,
            device_id=(to_row, to_col), device_id_type=MESH,
        )

    def in_half(i):
        return half * mid + lax.rem(row + i // cols, mid), lax.rem(col + i, cols)

    barrier = pltpu.get_barrier_semaphore()

    def greet(to_row, to_col):
        pl.semaphore_signal(barrier, inc=1, device_id=(to_row, to_col), device_id_type=MESH)

    def is_inner(at_row):
        return (at_row == mid - 1) | (at_row == mid)

    @pl.when(raw)
    def _():
        greet(mirror, col)

    even = lax.rem(col, 2) == 0
    greet(pair, col + (is_inner(pair) & even).astype(jnp.int32))

    @pl.loop(1, near + 1)
    def _(i):
        to_row, to_col = in_half(i)

        @pl.when(jnp.logical_not(is_inner(to_row) & (lax.rem(to_col, 2) == 0)))
        def _():
            greet(to_row, to_col)

    smalls = [
        pltpu.make_async_copy(src, dst, small_sem.at[i])
        for i, (src, dst) in enumerate(
            ((class_in, class_ref), (mask_in, mask_ref), (eff_in, eff_ref), (cond_in, cond_ref))
        )
    ]
    for copy in smalls:
        copy.start()
    for c in range(cols):
        pltpu.make_async_copy(
            frames.at[:, :, c * LANES : (c + 1) * LANES], x.at[c, 0:local], load_sem
        ).start()

    proxy = inner & jnp.logical_not(even)

    far_rows = pl.ds(aligned(other * half_rows, PAD), half_rows)
    near_rows = pl.ds(aligned(half * half_rows, PAD), half_rows)

    def raw_copy(c):
        return remote(
            frames.at[0:GROUP, far_rows, c * LANES : (c + 1) * LANES],
            x.at[c, local : local + GROUP, far_rows],
            raw_send, raw_recv, mirror, col,
        )

    @pl.when(raw)
    def _():
        pl.semaphore_wait(barrier, 1)
        for c in range(EARLY):
            raw_copy(c).start()

    for copy in smalls:
        copy.wait()
    classes = class_ref[...]
    maskf = mask_ref[...].astype(jnp.float32)
    eff = jnp.zeros(classes.shape, jnp.float32)
    cond = jnp.zeros(classes.shape, jnp.float32)
    for k in range(eff_ref.shape[0]):
        eff = jnp.where(classes == k, eff_ref[k], eff)
        cond = jnp.where(classes == k, cond_ref[k], cond)

    def tile_of(at_row, at_col):
        return coef.at[at_col, :, pl.ds(aligned(PAD + at_row * tile_rows, PAD), tile_rows)]

    own_rows = pl.ds(aligned(PAD + row * tile_rows, PAD), tile_rows)
    coef[col, 0, own_rows] = lateral_rate * cond * maskf
    coef[col, 1, own_rows] = flux_factor * eff * maskf
    for c in range(cols):
        for k in range(2):
            coef[c, k, 0:PAD] = jnp.zeros((PAD, LANES), jnp.float32)
            coef[c, k, PAD + height : 2 * PAD + height] = jnp.zeros((PAD, LANES), jnp.float32)

    @pl.when(jnp.logical_not(raw))
    def _():
        pl.semaphore_wait(barrier, near + 1 + proxy.astype(jnp.int32))

    @pl.when(proxy)
    def _():
        pl.semaphore_signal(ready, inc=1, device_id=(row, col - 1), device_id_type=MESH)

    @pl.when(raw)
    def _():
        pl.semaphore_wait(ready, 1)


    own_tile, pair_tile = tile_of(row, col), tile_of(pair, col)
    remote(own_tile, own_tile, coef_send.at[0], pair_recv, pair, col).start()

    @pl.loop(1, near + 1)
    def _(i):
        to_row, to_col = in_half(i)
        remote(own_tile, own_tile, coef_send.at[1], near_recv, to_row, to_col).start()

    edge_copy = remote(edge_out, edge_in, edge_send, edge_recv, mirror, col)

    @pl.when(raw)
    def _():
        for c in range(EARLY, cols):
            raw_copy(c).start()

    wait_for(x.at[:, 0:local], load_sem)
    lines = x.reshape(cols, (local + GROUP) * height, LANES)

    def line(c, group, at):
        return lines[c, pl.ds(group * (GROUP * height) + at, GROUP, stride=height), :]

    @pl.when(raw)
    def _():
        for k in range(halo):
            for c in range(cols):
                edge_out[k, c] = line(c, 0, half_rows - halo * other + k)
        edge_copy.start()

    def fill_mix():
        block = tile_cols

        @pl.loop(0, total // block)
        def _(k):
            shape = (block, total)
            earlier = lax.broadcasted_iota(jnp.int32, shape, 0) + k * block
            later = lax.broadcasted_iota(jnp.int32, shape, 1)
            lagged = (later - earlier).astype(jnp.float32)
            mix = weights(lagged) - weights(lagged - 1.0)
            high = mix.astype(jnp.bfloat16)
            at = pl.ds(aligned(k * block, block), block)
            mix_ref[0, at] = high
            mix_ref[1, at] = (mix - high.astype(jnp.float32)).astype(jnp.bfloat16)

    lane = lax.broadcasted_iota(jnp.int32, (GROUP, LANES), 1)
    leftmost, rightmost = lane == 0, lane == LANES - 1
    nothing = jnp.zeros((GROUP, LANES), jnp.float32)

    def spread(c, which, at):
        return coef[c, which, pl.ds(at, GROUP, stride=0), :]

    def relax(source_ref, base, begin, end, unroll, store):

        @pl.loop(begin, end, step=unroll)
        def _(i):
            lines_at = [[source_ref[i + k, c] for c in range(cols)] for k in range(-1, unroll + 1)]
            for k in range(unroll):
                above, center, below = lines_at[k : k + 3]
                ahead = [pltpu.roll(v, 1, 1) for v in center]
                behind = [pltpu.roll(v, LANES - 1, 1) for v in center]
                for c in range(cols):
                    left = jnp.where(leftmost, ahead[c - 1] if c else nothing, ahead[c])
                    right = jnp.where(rightmost, behind[c + 1] if c + 1 < cols else nothing, behind[c])
                    laplace = below[c] + above[c] + right + left - 4.0 * center[c]
                    store(i + k, c, center[c] + spread(c, 0, base + i + k) * laplace)

    def keep(ref):
        def store(i, c, value):
            ref[i, c] = value
        return store

    def sweep(side, group, edge, store_last):
        span = half_rows + 2 * halo
        base = side * half_rows - halo + PAD
        for k in range(halo):
            at = half_rows - halo * side + k
            for c in range(cols):
                first[(half_rows + halo) * side + k, c] = nothing
                first[(half_rows + halo) * (1 - side) + k, c] = spread(c, 1, at + PAD) * edge(k, c, at)
        for c in range(cols):
            second[0, c] = nothing
            second[span - 1, c] = nothing

        @pl.loop(0, half_rows, step=LINES)
        def _(j):
            for k in range(LINES):
                at = half_rows * side + j + k
                for c in range(cols):
                    first[halo + j + k, c] = spread(c, 1, at + PAD) * line(c, group, at)

        relax(first, base, 1, span - 1, ROWS, keep(second))
        relax(second, base, 1, span - 1, ROWS, keep(first))
        relax(first, base, halo, span - halo, LINES, store_last)

    def sweep_tile(side, group, tile):
        begin = side * half_rows + tile * tile_rows - halo
        span = tile_rows + 2 * halo
        for k in range(span):
            at = begin + k
            for c in range(cols):
                first[k, c] = spread(c, 1, at + PAD) * line(c, group, lax.rem(at + height, height))
        for c in range(cols):
            second[0, c] = nothing
            second[span - 1, c] = nothing

        def store(i, c, value):
            at = pl.ds(aligned(group * GROUP, GROUP), GROUP)
            done[side * mid + tile, c, i - halo, at, :] = value

        base = begin + PAD
        relax(first, base, 1, span - 1, (span - 2) // 2, keep(second))
        relax(second, base, 1, span - 1, (span - 2) // 2, keep(first))
        relax(first, base, halo, span - halo, tile_rows, store)

    def sweep_own(side, group):
        def store(i, c, value):
            j = i - halo
            at = pl.ds(aligned(group * GROUP, GROUP), GROUP)
            done[side * mid + j // tile_rows, c, lax.rem(j, tile_rows), at, :] = value

        sweep(side, group, lambda k, c, at: line(c, group, at), store)

    def sweep_raw():
        def store(i, c, value):
            j = i - halo
            done_far[j // tile_rows, c, lax.rem(j, tile_rows), :, :] = value

        sweep(half, local // GROUP, lambda k, c, at: edge_in[k, c], store)

    groups = local // GROUP

    def rows_of(q):
        return pl.ds(q * part, part)

    def slots(at, count):
        return pl.ds(aligned(at, GROUP), count)

    fill_mix()

    wait_for(pair_tile, pair_recv)

    @pl.loop(1, near + 1)
    def _(i):
        to_row, to_col = in_half(i)
        remote(pair_tile, pair_tile, coef_send.at[2], far_recv, to_row, to_col).start()

    def tiles(count):
        return held.at[pl.ds(0, count), pl.ds(0, 2 * tile_rows)]

    wait_for(tiles(near), near_recv)
    wait_for(tiles(near), far_recv)

    own_slots = slots(source * local, local)

    def across(i):
        return other * mid + lax.rem(row + i // cols, mid), lax.rem(col + i, cols)

    def send_near(q):
        pltpu.make_async_copy(
            done.at[row, col, rows_of(q)], held.at[rows_of(q), own_slots], recv_sem.at[q]
        ).start()

        @pl.loop(1, near + 1)
        def _(i):
            to_row, to_col = in_half(i)
            remote(
                done.at[to_row, to_col, rows_of(q)], held.at[rows_of(q), own_slots],
                near_send, recv_sem.at[q], to_row, to_col,
            ).start()

    def cross_copy(q, skip, to_row, to_col):
        count = local - skip
        return remote(
            done.at[to_row, to_col, rows_of(q), pl.ds(skip, count)],
            held.at[rows_of(q), slots(source * local + skip, count)],
            cross_send, recv_sem.at[q], to_row, to_col,
        )

    def send_cross(q):
        @pl.loop(0, near + 1)
        def _(i):
            cross_copy(q, 0, *across(i)).start()

    @pl.when(raw)
    def _():
        @pl.loop(0, mid)
        def _(t):
            tile = lax.rem(row + t, mid)
            to_row = other * mid + tile

            @pl.loop(1, groups)
            def _(g):
                sweep_tile(other, g, tile)

            @pl.loop(0, steps)
            def _(q):
                @pl.loop(0, cols)
                def _(i):
                    cross_copy(q, GROUP, to_row, lax.rem(col + i, cols)).start()

    @pl.when(jnp.logical_not(raw))
    def _():
        @pl.loop(0, groups)
        def _(g):
            sweep_own(other, g)

    @pl.when(inner & jnp.logical_not(raw))
    def _():
        @pl.loop(0, steps)
        def _(q):
            send_cross(q)

    @pl.loop(0, groups)
    def _(g):
        sweep_own(half, g)

    @pl.loop(0, steps)
    def _(q):
        @pl.when(jnp.logical_not(inner))
        def _():
            send_cross(q)

        send_near(q)

    @pl.when(raw)
    def _():
        wait_for(x.at[:, local : local + GROUP, near_rows], raw_recv)
        edge_copy.wait_recv()
        sweep_raw()
        there = slots((mirror * cols + col) * local, GROUP)

        @pl.loop(0, steps)
        def _(q):
            pltpu.make_async_copy(
                done_far.at[row - half * mid, col, rows_of(q)], held.at[rows_of(q), there],
                recv_sem.at[q],
            ).start()

            @pl.loop(1, near + 1)
            def _(i):
                to_row, to_col = in_half(i)
                remote(
                    done_far.at[to_row - half * mid, to_col, rows_of(q)],
                    held.at[rows_of(q), there],
                    relay_send, recv_sem.at[q], to_row, to_col,
                ).start()

    @pl.loop(0, steps - 1)
    def _(q):
        wait_for(held.at[rows_of(q)], recv_sem.at[q])
        convolve(held, mix_ref, flux, q * part, part)

    wait_for(held.at[rows_of(steps - 1)], recv_sem.at[steps - 1])

    wait_for(own_tile, coef_send.at[0])
    wait_for(tiles(near), coef_send.at[1])
    wait_for(tiles(near), coef_send.at[2])
    wait_for(held.at[:, pl.ds(0, near * local)], near_send)

    @pl.when(raw)
    def _():
        wait_for(x.at[:, local : local + GROUP, far_rows], raw_send)
        edge_copy.wait_send()
        wait_for(held.at[:, pl.ds(0, (near + 1) * (local - GROUP))], cross_send)
        wait_for(held.at[:, pl.ds(0, near * GROUP)], relay_send)

    @pl.when(jnp.logical_not(raw))
    def _():
        wait_for(held.at[:, pl.ds(0, (near + 1) * local)], cross_send)


def convolve(held, mix_ref, flux, begin, count):
    total, width = held.shape[1], held.shape[2]
    x = jnp.transpose(held[pl.ds(begin, count)], (0, 2, 1)).reshape(count * width, total)
    high = x.astype(jnp.bfloat16)
    low = (x - high.astype(jnp.float32)).astype(jnp.bfloat16)
    cut = total // 2
    for a, b in ((0, cut), (cut, total)):
        out = jnp.dot(high[:, :b], mix_ref[0, :b, a:b], preferred_element_type=jnp.float32)
        out += jnp.dot(low[:, :b], mix_ref[0, :b, a:b], preferred_element_type=jnp.float32)
        out += jnp.dot(high[:, :b], mix_ref[1, :b, a:b], preferred_element_type=jnp.float32)
        flux[pl.ds(begin, count), :, a:b] = out.reshape(count, width, b - a)


def finish_kernel(part, held, flux, mix_ref, out, last, sem):
    rows = held.shape[0]
    ready = rows - part
    early = pltpu.make_async_copy(flux.at[0:ready], out.at[0:ready], sem.at[0])
    early.start()
    convolve(held.at[ready:rows], mix_ref, last, 0, part)
    late = pltpu.make_async_copy(last, out.at[ready:rows], sem.at[1])
    late.start()
    early.wait()
    late.wait()


def per_device(frames, class_index, surface_mask, effusivity, conductivity):
    rows = lax.axis_size("row")
    cols = lax.axis_size("col")
    local, height, width = frames.shape
    tile_rows, tile_cols = height // rows, width // cols
    total = local * rows * cols
    near = rows // 2 * cols - 1
    fits = (
        rows % 2 == 0 and cols % 2 == 0 and local % (2 * GROUP) == 0 and tile_rows % PAD == 0
        and tile_rows % STEPS == 0 and tile_cols == LANES and total % (2 * LANES) == 0
        and near <= tile_rows and cols >= EARLY and 2 * tile_rows <= total
        and height // 2 % LINES == 0 and (height // 2 + 2 * PASSES - 2) % ROWS == 0
    )
    if not fits:
        return plain_device(frames, class_index, surface_mask, effusivity, conductivity)
    half_rows, span = height // 2, height // 2 + 2 * PASSES
    vmem = pl.BlockSpec(memory_space=pltpu.VMEM)
    hbm = pl.BlockSpec(memory_space=pltpu.HBM)
    dma = pltpu.SemaphoreType.DMA
    f32 = jnp.float32
    arguments = (frames, class_index, surface_mask, effusivity, conductivity)
    held, flux, mix = pl.pallas_call(
        functools.partial(gather_kernel, rows, cols, tile_rows, tile_cols, local, height, STEPS),
        out_shape=(
            jax.ShapeDtypeStruct((tile_rows, total, LANES), f32),
            jax.ShapeDtypeStruct((tile_rows, tile_cols, total), f32),
            jax.ShapeDtypeStruct((2, total, total), jnp.bfloat16),
        ),
        in_specs=[hbm] * 5,
        out_specs=(vmem, vmem, vmem),
        scratch_shapes=[
            pltpu.VMEM((cols, local + GROUP, height, LANES), f32),
            pltpu.VMEM((cols, 2, height + 2 * PAD, LANES), f32),
            pltpu.VMEM((rows, cols, tile_rows, local, LANES), f32),
            pltpu.VMEM((rows // 2, cols, tile_rows, GROUP, LANES), f32),
            pltpu.VMEM((span, cols, GROUP, LANES), f32),
            pltpu.VMEM((span, cols, GROUP, LANES), f32),
            pltpu.VMEM((PASSES, cols, GROUP, LANES), f32),
            pltpu.VMEM((PASSES, cols, GROUP, LANES), f32),
            pltpu.VMEM((tile_rows, tile_cols), jnp.int32),
            pltpu.VMEM((tile_rows, tile_cols), jnp.int32),
            pltpu.SMEM(effusivity.shape, f32),
            pltpu.SMEM(conductivity.shape, f32),
            dma, dma((4,)), dma((3,)), dma, dma, dma,
            dma, dma, dma, dma,
            dma, dma, dma, dma((STEPS,)), pltpu.SemaphoreType.REGULAR,
        ],
        compiler_params=pltpu.CompilerParams(
            collective_id=0, has_side_effects=True, vmem_limit_bytes=VMEM_GATHER
        ),
        name="gather",
    )(*(pltpu.with_memory_space_constraint(a, pltpu.HBM) for a in arguments))
    part = tile_rows // STEPS
    return pl.pallas_call(
        functools.partial(finish_kernel, part),
        out_shape=jax.ShapeDtypeStruct((tile_rows, tile_cols, total), f32),
        in_specs=[vmem, vmem, vmem],
        out_specs=hbm,
        scratch_shapes=[pltpu.VMEM((part, tile_cols, total), f32), dma((2,))],
        compiler_params=pltpu.CompilerParams(vmem_limit_bytes=24 * 2**20),
        name="finish",
    )(held, flux, mix)


def solution(mesh):
    in_specs = (P(("row", "col"), None, None), P("row", "col"), P("row", "col"), P(), P())
    out_specs = P("row", "col", None)
    return jax.shard_map(
        per_device, mesh=mesh, in_specs=in_specs, out_specs=out_specs, check_vma=False
    )
```

```python
import functools
import jax
import jax.numpy as jnp
from jax import lax
from jax.experimental import pallas as pl
from jax.experimental.pallas import tpu as pltpu
from jax.sharding import PartitionSpec as P

PASSES = 3
PAD = 8
GROUP = 8
LANES = 128
STEPS = 4
ROWS = 12
LINES = 16
EARLY = 1
VMEM_GATHER = 40 * 2**20
MESH = pl.DeviceIdType.MESH

flux_factor = 1.1283791670955126
lateral_rate = 0.24


def extended(block, sides, width):
    for axis, dim in sides:
        count = lax.axis_size(axis)
        forward = [(i, i + 1) for i in range(count - 1)]
        backward = [(target, source) for source, target in forward]
        low = lax.ppermute(
            lax.slice_in_dim(block, block.shape[dim] - width, None, axis=dim), axis, forward
        )
        high = lax.ppermute(lax.slice_in_dim(block, 0, width, axis=dim), axis, backward)
        block = jnp.concatenate([low, block, high], axis=dim)
    return block


def weights(lagged):
    clipped = jnp.maximum(lagged, 0.0)
    return jnp.where(lagged >= 0.0, 1.0 / (jnp.sqrt(clipped) + jnp.sqrt(clipped + 1.0)), 0.0)


def kernel_from(later, earlier):
    lagged = (later[:, None] - earlier[None, :]).astype(jnp.float32)
    return weights(lagged) - weights(lagged - 1.0)


def relax_once(padded, lateral):
    center = padded[1:-1, 1:-1]
    laplace = (
        padded[2:, 1:-1] + padded[:-2, 1:-1] + padded[1:-1, 2:] + padded[1:-1, :-2] - 4.0 * center
    )
    return center + lateral[:, :, None] * laplace


def plain_device(frames, class_index, surface_mask, effusivity, conductivity):
    row_count = lax.axis_size("row")
    col_count = lax.axis_size("col")
    local_frames, height, width = frames.shape
    tile_rows = height // row_count
    tile_cols = width // col_count
    total_frames = local_frames * row_count * col_count
    frame_ids = jnp.arange(total_frames, dtype=jnp.int32)
    contract = (((0,), (1,)), ((), ()))
    kernel = kernel_from(frame_ids, frame_ids)
    blocks = frames.reshape(local_frames, row_count, tile_rows, col_count, tile_cols)
    blocks = blocks.transpose(0, 1, 3, 2, 4).reshape(
        local_frames, row_count * col_count, tile_rows, tile_cols
    )
    convolved = lax.dot_general(
        lax.all_to_all(blocks, ("row", "col"), split_axis=1, concat_axis=0, tiled=True)[:, 0],
        kernel,
        contract,
        precision=lax.Precision.HIGHEST,
    )
    classes = jnp.arange(effusivity.shape[0], dtype=jnp.int32)
    matches = (class_index[:, :, None] == classes[None, None, :]).astype(jnp.float32)
    maskf = surface_mask.astype(jnp.float32)
    gain = flux_factor * jnp.sum(matches * effusivity, axis=-1) * maskf
    lateral = lateral_rate * jnp.sum(matches * conductivity, axis=-1) * maskf
    heat_flux = convolved * gain[:, :, None]
    padded = extended(heat_flux, (("row", 0), ("col", 1)), PASSES)
    lateral_wide = extended(lateral, (("row", 0), ("col", 1)), PASSES - 1)
    for pass_index in range(PASSES):
        margin = PASSES - 1 - pass_index
        offset = PASSES - 1 - margin
        lateral_part = lateral_wide[
            offset : offset + tile_rows + 2 * margin, offset : offset + tile_cols + 2 * margin
        ]
        padded = relax_once(padded, lateral_part)
    return padded


def gather_kernel(
    rows, cols, tile_rows, tile_cols, local, height, steps,
    frames, class_in, mask_in, eff_in, cond_in,
    held, flux, mix_ref,
    x, coef, done, done_far, first, second, edge_out, edge_in,
    class_ref, mask_ref, eff_ref, cond_ref,
    load_sem, small_sem, coef_send, near_recv, pair_recv, far_recv,
    raw_send, raw_recv, edge_send, edge_recv,
    near_send, cross_send, relay_send, recv_sem, ready,
):
    row, col = lax.axis_index("row"), lax.axis_index("col")
    mid = rows // 2
    half = row // mid
    other = 1 - half
    half_rows = height // 2
    total = rows * cols * local
    halo = PASSES
    near = mid * cols - 1
    part = tile_rows // steps
    source = row * cols + col
    mirror, pair = rows - 1 - row, lax.rem(row + mid, rows)
    inner = (row == mid - 1) | (row == mid)
    raw = inner & (lax.rem(col, 2) == 0)

    def wait_for(ref, sem):
        pltpu.make_async_copy(ref, ref, sem).wait()

    def aligned(value, unit):
        return pl.multiple_of(value, unit)

    def remote(src, dst, send, recv, to_row, to_col):
        return pltpu.make_async_remote_copy(
            src_ref=src, dst_ref=dst, send_sem=send, recv_sem=recv,
            device_id=(to_row, to_col), device_id_type=MESH,
        )

    def turn(i):
        return lax.rem(col + lax.rem(i, cols // 2) * 2 + lax.rem(i // (cols // 2), 2), cols)

    def in_half(i):
        return half * mid + lax.rem(row + i // cols, mid), lax.rem(col + i, cols)

    barrier = pltpu.get_barrier_semaphore()

    def greet(to_row, to_col):
        pl.semaphore_signal(barrier, inc=1, device_id=(to_row, to_col), device_id_type=MESH)

    def is_inner(at_row):
        return (at_row == mid - 1) | (at_row == mid)

    @pl.when(raw)
    def _():
        greet(mirror, col)

    even = lax.rem(col, 2) == 0
    greet(pair, col + (is_inner(pair) & even).astype(jnp.int32))

    @pl.loop(1, near + 1)
    def _(i):
        to_row, to_col = in_half(i)

        @pl.when(jnp.logical_not(is_inner(to_row) & (lax.rem(to_col, 2) == 0)))
        def _():
            greet(to_row, to_col)

    smalls = [
        pltpu.make_async_copy(src, dst, small_sem.at[i])
        for i, (src, dst) in enumerate(
            ((class_in, class_ref), (mask_in, mask_ref), (eff_in, eff_ref), (cond_in, cond_ref))
        )
    ]
    for copy in smalls:
        copy.start()
    for c in range(cols):
        pltpu.make_async_copy(
            frames.at[:, :, c * LANES : (c + 1) * LANES], x.at[c, 0:local], load_sem
        ).start()

    proxy = inner & jnp.logical_not(even)

    far_rows = pl.ds(aligned(other * half_rows, PAD), half_rows)
    near_rows = pl.ds(aligned(half * half_rows, PAD), half_rows)

    def raw_copy(c):
        return remote(
            frames.at[0:GROUP, far_rows, c * LANES : (c + 1) * LANES],
            x.at[c, local : local + GROUP, far_rows],
            raw_send, raw_recv, mirror, col,
        )

    @pl.when(raw)
    def _():
        pl.semaphore_wait(barrier, 1)
        for c in range(EARLY):
            raw_copy(c).start()

    for copy in smalls:
        copy.wait()
    classes = class_ref[...]
    maskf = mask_ref[...].astype(jnp.float32)
    eff = jnp.zeros(classes.shape, jnp.float32)
    cond = jnp.zeros(classes.shape, jnp.float32)
    for k in range(eff_ref.shape[0]):
        eff = jnp.where(classes == k, eff_ref[k], eff)
        cond = jnp.where(classes == k, cond_ref[k], cond)

    def tile_of(at_row, at_col):
        return coef.at[at_col, :, pl.ds(aligned(PAD + at_row * tile_rows, PAD), tile_rows)]

    own_rows = pl.ds(aligned(PAD + row * tile_rows, PAD), tile_rows)
    coef[col, 0, own_rows] = lateral_rate * cond * maskf
    coef[col, 1, own_rows] = flux_factor * eff * maskf
    for c in range(cols):
        for k in range(2):
            coef[c, k, 0:PAD] = jnp.zeros((PAD, LANES), jnp.float32)
            coef[c, k, PAD + height : 2 * PAD + height] = jnp.zeros((PAD, LANES), jnp.float32)

    @pl.when(jnp.logical_not(raw))
    def _():
        pl.semaphore_wait(barrier, near + 1 + proxy.astype(jnp.int32))

    @pl.when(proxy)
    def _():
        pl.semaphore_signal(ready, inc=1, device_id=(row, col - 1), device_id_type=MESH)

    @pl.when(raw)
    def _():
        pl.semaphore_wait(ready, 1)


    own_tile, pair_tile = tile_of(row, col), tile_of(pair, col)
    remote(own_tile, own_tile, coef_send.at[0], pair_recv, pair, col).start()

    @pl.loop(1, near + 1)
    def _(i):
        to_row, to_col = in_half(i)
        remote(own_tile, own_tile, coef_send.at[1], near_recv, to_row, to_col).start()

    edge_copy = remote(edge_out, edge_in, edge_send, edge_recv, mirror, col)

    @pl.when(raw)
    def _():
        for c in range(EARLY, cols):
            raw_copy(c).start()

    wait_for(x.at[:, 0:local], load_sem)
    lines = x.reshape(cols, (local + GROUP) * height, LANES)

    def line(c, group, at):
        return lines[c, pl.ds(group * (GROUP * height) + at, GROUP, stride=height), :]

    @pl.when(raw)
    def _():
        for k in range(halo):
            for c in range(cols):
                edge_out[k, c] = line(c, 0, half_rows - halo * other + k)
        edge_copy.start()

    def fill_mix():
        block = tile_cols

        @pl.loop(0, total // block)
        def _(k):
            shape = (block, total)
            earlier = lax.broadcasted_iota(jnp.int32, shape, 0) + k * block
            later = lax.broadcasted_iota(jnp.int32, shape, 1)
            lagged = (later - earlier).astype(jnp.float32)
            mix = weights(lagged) - weights(lagged - 1.0)
            high = mix.astype(jnp.bfloat16)
            at = pl.ds(aligned(k * block, block), block)
            mix_ref[0, at] = high
            mix_ref[1, at] = (mix - high.astype(jnp.float32)).astype(jnp.bfloat16)

    lane = lax.broadcasted_iota(jnp.int32, (GROUP, LANES), 1)
    leftmost, rightmost = lane == 0, lane == LANES - 1
    nothing = jnp.zeros((GROUP, LANES), jnp.float32)

    def spread(c, which, at):
        return coef[c, which, pl.ds(at, GROUP, stride=0), :]

    def relax(source_ref, base, begin, end, unroll, store):

        @pl.loop(begin, end, step=unroll)
        def _(i):
            lines_at = [[source_ref[i + k, c] for c in range(cols)] for k in range(-1, unroll + 1)]
            for k in range(unroll):
                above, center, below = lines_at[k : k + 3]
                ahead = [pltpu.roll(v, 1, 1) for v in center]
                behind = [pltpu.roll(v, LANES - 1, 1) for v in center]
                for c in range(cols):
                    left = jnp.where(leftmost, ahead[c - 1] if c else nothing, ahead[c])
                    right = jnp.where(rightmost, behind[c + 1] if c + 1 < cols else nothing, behind[c])
                    laplace = below[c] + above[c] + right + left - 4.0 * center[c]
                    store(i + k, c, center[c] + spread(c, 0, base + i + k) * laplace)

    def keep(ref):
        def store(i, c, value):
            ref[i, c] = value
        return store

    def sweep(side, group, edge, store_last):
        span = half_rows + 2 * halo
        base = side * half_rows - halo + PAD
        for k in range(halo):
            at = half_rows - halo * side + k
            for c in range(cols):
                first[(half_rows + halo) * side + k, c] = nothing
                first[(half_rows + halo) * (1 - side) + k, c] = spread(c, 1, at + PAD) * edge(k, c, at)
        for c in range(cols):
            second[0, c] = nothing
            second[span - 1, c] = nothing

        @pl.loop(0, half_rows, step=LINES)
        def _(j):
            for k in range(LINES):
                at = half_rows * side + j + k
                for c in range(cols):
                    first[halo + j + k, c] = spread(c, 1, at + PAD) * line(c, group, at)

        relax(first, base, 1, span - 1, ROWS, keep(second))
        relax(second, base, 1, span - 1, ROWS, keep(first))
        relax(first, base, halo, span - halo, LINES, store_last)

    def sweep_tile(side, group, tile):
        begin = side * half_rows + tile * tile_rows - halo
        span = tile_rows + 2 * halo
        for k in range(span):
            at = begin + k
            for c in range(cols):
                first[k, c] = spread(c, 1, at + PAD) * line(c, group, lax.rem(at + height, height))
        for c in range(cols):
            second[0, c] = nothing
            second[span - 1, c] = nothing

        def store(i, c, value):
            at = pl.ds(aligned(group * GROUP, GROUP), GROUP)
            done[side * mid + tile, c, i - halo, at, :] = value

        base = begin + PAD
        relax(first, base, 1, span - 1, (span - 2) // 2, keep(second))
        relax(second, base, 1, span - 1, (span - 2) // 2, keep(first))
        relax(first, base, halo, span - halo, tile_rows, store)

    def sweep_own(side, group):
        def store(i, c, value):
            j = i - halo
            at = pl.ds(aligned(group * GROUP, GROUP), GROUP)
            done[side * mid + j // tile_rows, c, lax.rem(j, tile_rows), at, :] = value

        sweep(side, group, lambda k, c, at: line(c, group, at), store)

    def sweep_raw():
        def store(i, c, value):
            j = i - halo
            done_far[j // tile_rows, c, lax.rem(j, tile_rows), :, :] = value

        sweep(half, local // GROUP, lambda k, c, at: edge_in[k, c], store)

    groups = local // GROUP

    def rows_of(q):
        return pl.ds(q * part, part)

    def slots(at, count):
        return pl.ds(aligned(at, GROUP), count)

    fill_mix()

    wait_for(pair_tile, pair_recv)

    @pl.loop(1, near + 1)
    def _(i):
        to_row, to_col = in_half(i)
        remote(pair_tile, pair_tile, coef_send.at[2], far_recv, to_row, to_col).start()

    def tiles(count):
        return held.at[pl.ds(0, count), pl.ds(0, 2 * tile_rows)]

    wait_for(tiles(near), near_recv)
    wait_for(tiles(near), far_recv)

    own_slots = slots(source * local, local)

    def across(i):
        return other * mid + lax.rem(row + i // cols, mid), turn(i)

    def send_near(q):
        pltpu.make_async_copy(
            done.at[row, col, rows_of(q)], held.at[rows_of(q), own_slots], recv_sem.at[q]
        ).start()

        @pl.loop(1, near + 1)
        def _(i):
            to_row, to_col = in_half(near + 1 - i)
            remote(
                done.at[to_row, to_col, rows_of(q)], held.at[rows_of(q), own_slots],
                near_send, recv_sem.at[q], to_row, to_col,
            ).start()

    def cross_copy(q, skip, to_row, to_col):
        count = local - skip
        return remote(
            done.at[to_row, to_col, rows_of(q), pl.ds(skip, count)],
            held.at[rows_of(q), slots(source * local + skip, count)],
            cross_send, recv_sem.at[q], to_row, to_col,
        )

    def send_cross(q):
        @pl.loop(0, near + 1)
        def _(i):
            cross_copy(q, 0, *across(i)).start()

    @pl.when(raw)
    def _():
        @pl.loop(0, mid)
        def _(t):
            tile = lax.rem(row + t, mid)
            to_row = other * mid + tile

            @pl.loop(1, groups)
            def _(g):
                sweep_tile(other, g, tile)

            @pl.loop(0, steps)
            def _(q):
                @pl.loop(0, cols)
                def _(i):
                    cross_copy(q, GROUP, to_row, turn(i)).start()

    @pl.when(jnp.logical_not(raw))
    def _():
        @pl.loop(0, groups)
        def _(g):
            sweep_own(other, g)

    @pl.when(inner & jnp.logical_not(raw))
    def _():
        @pl.loop(0, steps)
        def _(q):
            send_cross(q)

    @pl.loop(0, groups)
    def _(g):
        sweep_own(half, g)

    @pl.loop(0, steps)
    def _(q):
        @pl.when(jnp.logical_not(inner))
        def _():
            send_cross(q)

        send_near(q)

    @pl.when(raw)
    def _():
        wait_for(x.at[:, local : local + GROUP, near_rows], raw_recv)
        edge_copy.wait_recv()
        sweep_raw()
        there = slots((mirror * cols + col) * local, GROUP)

        @pl.loop(0, steps)
        def _(q):
            pltpu.make_async_copy(
                done_far.at[row - half * mid, col, rows_of(q)], held.at[rows_of(q), there],
                recv_sem.at[q],
            ).start()

            @pl.loop(1, near + 1)
            def _(i):
                to_row, to_col = in_half(i)
                remote(
                    done_far.at[to_row - half * mid, to_col, rows_of(q)],
                    held.at[rows_of(q), there],
                    relay_send, recv_sem.at[q], to_row, to_col,
                ).start()

    @pl.loop(0, steps - 1)
    def _(q):
        wait_for(held.at[rows_of(q)], recv_sem.at[q])
        convolve(held, mix_ref, flux, q * part, part)

    wait_for(held.at[rows_of(steps - 1)], recv_sem.at[steps - 1])

    wait_for(own_tile, coef_send.at[0])
    wait_for(tiles(near), coef_send.at[1])
    wait_for(tiles(near), coef_send.at[2])
    wait_for(held.at[:, pl.ds(0, near * local)], near_send)

    @pl.when(raw)
    def _():
        wait_for(x.at[:, local : local + GROUP, far_rows], raw_send)
        edge_copy.wait_send()
        wait_for(held.at[:, pl.ds(0, (near + 1) * (local - GROUP))], cross_send)
        wait_for(held.at[:, pl.ds(0, near * GROUP)], relay_send)

    @pl.when(jnp.logical_not(raw))
    def _():
        wait_for(held.at[:, pl.ds(0, (near + 1) * local)], cross_send)


def convolve(held, mix_ref, flux, begin, count):
    total, width = held.shape[1], held.shape[2]
    x = jnp.transpose(held[pl.ds(begin, count)], (0, 2, 1)).reshape(count * width, total)
    high = x.astype(jnp.bfloat16)
    low = (x - high.astype(jnp.float32)).astype(jnp.bfloat16)
    cut = total // 2
    for a, b in ((0, cut), (cut, total)):
        out = jnp.dot(high[:, :b], mix_ref[0, :b, a:b], preferred_element_type=jnp.float32)
        out += jnp.dot(low[:, :b], mix_ref[0, :b, a:b], preferred_element_type=jnp.float32)
        out += jnp.dot(high[:, :b], mix_ref[1, :b, a:b], preferred_element_type=jnp.float32)
        flux[pl.ds(begin, count), :, a:b] = out.reshape(count, width, b - a)


def finish_kernel(part, held, flux, mix_ref, out, last, sem):
    rows = held.shape[0]
    ready = rows - part
    early = pltpu.make_async_copy(flux.at[0:ready], out.at[0:ready], sem.at[0])
    early.start()
    convolve(held.at[ready:rows], mix_ref, last, 0, part)
    late = pltpu.make_async_copy(last, out.at[ready:rows], sem.at[1])
    late.start()
    early.wait()
    late.wait()


def per_device(frames, class_index, surface_mask, effusivity, conductivity):
    rows = lax.axis_size("row")
    cols = lax.axis_size("col")
    local, height, width = frames.shape
    tile_rows, tile_cols = height // rows, width // cols
    total = local * rows * cols
    near = rows // 2 * cols - 1
    fits = (
        rows % 2 == 0 and cols % 2 == 0 and local % (2 * GROUP) == 0 and tile_rows % PAD == 0
        and tile_rows % STEPS == 0 and tile_cols == LANES and total % (2 * LANES) == 0
        and near <= tile_rows and cols >= EARLY and 2 * tile_rows <= total
        and height // 2 % LINES == 0 and (height // 2 + 2 * PASSES - 2) % ROWS == 0
    )
    if not fits:
        return plain_device(frames, class_index, surface_mask, effusivity, conductivity)
    half_rows, span = height // 2, height // 2 + 2 * PASSES
    vmem = pl.BlockSpec(memory_space=pltpu.VMEM)
    hbm = pl.BlockSpec(memory_space=pltpu.HBM)
    dma = pltpu.SemaphoreType.DMA
    f32 = jnp.float32
    arguments = (frames, class_index, surface_mask, effusivity, conductivity)
    held, flux, mix = pl.pallas_call(
        functools.partial(gather_kernel, rows, cols, tile_rows, tile_cols, local, height, STEPS),
        out_shape=(
            jax.ShapeDtypeStruct((tile_rows, total, LANES), f32),
            jax.ShapeDtypeStruct((tile_rows, tile_cols, total), f32),
            jax.ShapeDtypeStruct((2, total, total), jnp.bfloat16),
        ),
        in_specs=[hbm] * 5,
        out_specs=(vmem, vmem, vmem),
        scratch_shapes=[
            pltpu.VMEM((cols, local + GROUP, height, LANES), f32),
            pltpu.VMEM((cols, 2, height + 2 * PAD, LANES), f32),
            pltpu.VMEM((rows, cols, tile_rows, local, LANES), f32),
            pltpu.VMEM((rows // 2, cols, tile_rows, GROUP, LANES), f32),
            pltpu.VMEM((span, cols, GROUP, LANES), f32),
            pltpu.VMEM((span, cols, GROUP, LANES), f32),
            pltpu.VMEM((PASSES, cols, GROUP, LANES), f32),
            pltpu.VMEM((PASSES, cols, GROUP, LANES), f32),
            pltpu.VMEM((tile_rows, tile_cols), jnp.int32),
            pltpu.VMEM((tile_rows, tile_cols), jnp.int32),
            pltpu.SMEM(effusivity.shape, f32),
            pltpu.SMEM(conductivity.shape, f32),
            dma, dma((4,)), dma((3,)), dma, dma, dma,
            dma, dma, dma, dma,
            dma, dma, dma, dma((STEPS,)), pltpu.SemaphoreType.REGULAR,
        ],
        compiler_params=pltpu.CompilerParams(
            collective_id=0, has_side_effects=True, vmem_limit_bytes=VMEM_GATHER
        ),
        name="gather",
    )(*(pltpu.with_memory_space_constraint(a, pltpu.HBM) for a in arguments))
    part = tile_rows // STEPS
    return pl.pallas_call(
        functools.partial(finish_kernel, part),
        out_shape=jax.ShapeDtypeStruct((tile_rows, tile_cols, total), f32),
        in_specs=[vmem, vmem, vmem],
        out_specs=hbm,
        scratch_shapes=[pltpu.VMEM((part, tile_cols, total), f32), dma((2,))],
        compiler_params=pltpu.CompilerParams(vmem_limit_bytes=24 * 2**20),
        name="finish",
    )(held, flux, mix)


def solution(mesh):
    in_specs = (P(("row", "col"), None, None), P("row", "col"), P("row", "col"), P(), P())
    out_specs = P("row", "col", None)
    return jax.shard_map(
        per_device, mesh=mesh, in_specs=in_specs, out_specs=out_specs, check_vma=False
    )
```

```python
import functools
import jax
import jax.numpy as jnp
from jax import lax
from jax.experimental import pallas as pl
from jax.experimental.pallas import tpu as pltpu
from jax.sharding import PartitionSpec as P

PASSES = 3
PAD = 8
GROUP = 8
LANES = 128
STEPS = 4
ROWS = 12
LINES = 16
EARLY = 1
VMEM_GATHER = 40 * 2**20
MESH = pl.DeviceIdType.MESH

flux_factor = 1.1283791670955126
lateral_rate = 0.24


def extended(block, sides, width):
    for axis, dim in sides:
        count = lax.axis_size(axis)
        forward = [(i, i + 1) for i in range(count - 1)]
        backward = [(target, source) for source, target in forward]
        low = lax.ppermute(
            lax.slice_in_dim(block, block.shape[dim] - width, None, axis=dim), axis, forward
        )
        high = lax.ppermute(lax.slice_in_dim(block, 0, width, axis=dim), axis, backward)
        block = jnp.concatenate([low, block, high], axis=dim)
    return block


def weights(lagged):
    clipped = jnp.maximum(lagged, 0.0)
    return jnp.where(lagged >= 0.0, 1.0 / (jnp.sqrt(clipped) + jnp.sqrt(clipped + 1.0)), 0.0)


def kernel_from(later, earlier):
    lagged = (later[:, None] - earlier[None, :]).astype(jnp.float32)
    return weights(lagged) - weights(lagged - 1.0)


def relax_once(padded, lateral):
    center = padded[1:-1, 1:-1]
    laplace = (
        padded[2:, 1:-1] + padded[:-2, 1:-1] + padded[1:-1, 2:] + padded[1:-1, :-2] - 4.0 * center
    )
    return center + lateral[:, :, None] * laplace


def plain_device(frames, class_index, surface_mask, effusivity, conductivity):
    row_count = lax.axis_size("row")
    col_count = lax.axis_size("col")
    local_frames, height, width = frames.shape
    tile_rows = height // row_count
    tile_cols = width // col_count
    total_frames = local_frames * row_count * col_count
    frame_ids = jnp.arange(total_frames, dtype=jnp.int32)
    contract = (((0,), (1,)), ((), ()))
    kernel = kernel_from(frame_ids, frame_ids)
    blocks = frames.reshape(local_frames, row_count, tile_rows, col_count, tile_cols)
    blocks = blocks.transpose(0, 1, 3, 2, 4).reshape(
        local_frames, row_count * col_count, tile_rows, tile_cols
    )
    convolved = lax.dot_general(
        lax.all_to_all(blocks, ("row", "col"), split_axis=1, concat_axis=0, tiled=True)[:, 0],
        kernel,
        contract,
        precision=lax.Precision.HIGHEST,
    )
    classes = jnp.arange(effusivity.shape[0], dtype=jnp.int32)
    matches = (class_index[:, :, None] == classes[None, None, :]).astype(jnp.float32)
    maskf = surface_mask.astype(jnp.float32)
    gain = flux_factor * jnp.sum(matches * effusivity, axis=-1) * maskf
    lateral = lateral_rate * jnp.sum(matches * conductivity, axis=-1) * maskf
    heat_flux = convolved * gain[:, :, None]
    padded = extended(heat_flux, (("row", 0), ("col", 1)), PASSES)
    lateral_wide = extended(lateral, (("row", 0), ("col", 1)), PASSES - 1)
    for pass_index in range(PASSES):
        margin = PASSES - 1 - pass_index
        offset = PASSES - 1 - margin
        lateral_part = lateral_wide[
            offset : offset + tile_rows + 2 * margin, offset : offset + tile_cols + 2 * margin
        ]
        padded = relax_once(padded, lateral_part)
    return padded


def gather_kernel(
    rows, cols, tile_rows, tile_cols, local, height, steps,
    frames, class_in, mask_in, eff_in, cond_in,
    held, flux, mix_ref,
    x, coef, done, done_far, first, second, edge_out, edge_in,
    class_ref, mask_ref, eff_ref, cond_ref,
    load_sem, small_sem, coef_send, near_recv, pair_recv, far_recv,
    raw_send, raw_recv, edge_send, edge_recv,
    near_send, cross_send, relay_send, recv_sem, ready,
):
    row, col = lax.axis_index("row"), lax.axis_index("col")
    mid = rows // 2
    half = row // mid
    other = 1 - half
    half_rows = height // 2
    total = rows * cols * local
    halo = PASSES
    near = mid * cols - 1
    part = tile_rows // steps
    source = row * cols + col
    mirror, pair = rows - 1 - row, lax.rem(row + mid, rows)
    inner = (row == mid - 1) | (row == mid)
    raw = inner & (lax.rem(col, 2) == 0)

    def wait_for(ref, sem):
        pltpu.make_async_copy(ref, ref, sem).wait()

    def aligned(value, unit):
        return pl.multiple_of(value, unit)

    def remote(src, dst, send, recv, to_row, to_col):
        return pltpu.make_async_remote_copy(
            src_ref=src, dst_ref=dst, send_sem=send, recv_sem=recv,
            device_id=(to_row, to_col), device_id_type=MESH,
        )

    def turn(i):
        return lax.rem(col + lax.rem(i, cols // 2) * 2 + lax.rem(i // (cols // 2), 2), cols)

    def in_half(i):
        return half * mid + lax.rem(row + i // cols, mid), lax.rem(col + i, cols)

    barrier = pltpu.get_barrier_semaphore()

    def greet(to_row, to_col):
        pl.semaphore_signal(barrier, inc=1, device_id=(to_row, to_col), device_id_type=MESH)

    def is_inner(at_row):
        return (at_row == mid - 1) | (at_row == mid)

    @pl.when(raw)
    def _():
        greet(mirror, col)

    even = lax.rem(col, 2) == 0
    greet(pair, col + (is_inner(pair) & even).astype(jnp.int32))

    @pl.loop(1, near + 1)
    def _(i):
        to_row, to_col = in_half(i)

        @pl.when(jnp.logical_not(is_inner(to_row) & (lax.rem(to_col, 2) == 0)))
        def _():
            greet(to_row, to_col)

    smalls = [
        pltpu.make_async_copy(src, dst, small_sem.at[i])
        for i, (src, dst) in enumerate(
            ((class_in, class_ref), (mask_in, mask_ref), (eff_in, eff_ref), (cond_in, cond_ref))
        )
    ]
    for copy in smalls:
        copy.start()
    for c in range(cols):
        pltpu.make_async_copy(
            frames.at[:, :, c * LANES : (c + 1) * LANES], x.at[c, 0:local], load_sem
        ).start()

    proxy = inner & jnp.logical_not(even)

    far_rows = pl.ds(aligned(other * half_rows, PAD), half_rows)
    near_rows = pl.ds(aligned(half * half_rows, PAD), half_rows)

    def raw_copy(c):
        return remote(
            frames.at[0:GROUP, far_rows, c * LANES : (c + 1) * LANES],
            x.at[c, local : local + GROUP, far_rows],
            raw_send, raw_recv, mirror, col,
        )

    @pl.when(raw)
    def _():
        pl.semaphore_wait(barrier, 1)
        for c in range(EARLY):
            raw_copy(c).start()

    for copy in smalls:
        copy.wait()
    classes = class_ref[...]
    maskf = mask_ref[...].astype(jnp.float32)
    eff = jnp.zeros(classes.shape, jnp.float32)
    cond = jnp.zeros(classes.shape, jnp.float32)
    for k in range(eff_ref.shape[0]):
        eff = jnp.where(classes == k, eff_ref[k], eff)
        cond = jnp.where(classes == k, cond_ref[k], cond)

    def tile_of(at_row, at_col):
        return coef.at[at_col, :, pl.ds(aligned(PAD + at_row * tile_rows, PAD), tile_rows)]

    own_rows = pl.ds(aligned(PAD + row * tile_rows, PAD), tile_rows)
    coef[col, 0, own_rows] = lateral_rate * cond * maskf
    coef[col, 1, own_rows] = flux_factor * eff * maskf
    for c in range(cols):
        for k in range(2):
            coef[c, k, 0:PAD] = jnp.zeros((PAD, LANES), jnp.float32)
            coef[c, k, PAD + height : 2 * PAD + height] = jnp.zeros((PAD, LANES), jnp.float32)

    @pl.when(jnp.logical_not(raw))
    def _():
        pl.semaphore_wait(barrier, near + 1 + proxy.astype(jnp.int32))

    @pl.when(proxy)
    def _():
        pl.semaphore_signal(ready, inc=1, device_id=(row, col - 1), device_id_type=MESH)

    @pl.when(raw)
    def _():
        pl.semaphore_wait(ready, 1)


    own_tile, pair_tile = tile_of(row, col), tile_of(pair, col)
    remote(own_tile, own_tile, coef_send.at[0], pair_recv, pair, col).start()

    @pl.loop(1, near + 1)
    def _(i):
        to_row, to_col = in_half(i)
        remote(own_tile, own_tile, coef_send.at[1], near_recv, to_row, to_col).start()

    edge_copy = remote(edge_out, edge_in, edge_send, edge_recv, mirror, col)

    @pl.when(raw)
    def _():
        for c in range(EARLY, cols):
            raw_copy(c).start()

    wait_for(x.at[:, 0:local], load_sem)
    lines = x.reshape(cols, x.shape[1] * height, LANES)

    def line(c, group, at):
        return lines[c, pl.ds(group * (GROUP * height) + at, GROUP, stride=height), :]

    @pl.when(raw)
    def _():
        for k in range(halo):
            for c in range(cols):
                edge_out[k, c] = line(c, 0, half_rows - halo * other + k)
        edge_copy.start()

    def fill_mix():
        block = tile_cols

        @pl.loop(0, total // block)
        def _(k):
            shape = (block, total)
            earlier = lax.broadcasted_iota(jnp.int32, shape, 0) + k * block
            later = lax.broadcasted_iota(jnp.int32, shape, 1)
            lagged = (later - earlier).astype(jnp.float32)
            mix = weights(lagged) - weights(lagged - 1.0)
            high = mix.astype(jnp.bfloat16)
            at = pl.ds(aligned(k * block, block), block)
            mix_ref[0, at] = high
            mix_ref[1, at] = (mix - high.astype(jnp.float32)).astype(jnp.bfloat16)

    lane = lax.broadcasted_iota(jnp.int32, (GROUP, LANES), 1)
    leftmost, rightmost = lane == 0, lane == LANES - 1
    nothing = jnp.zeros((GROUP, LANES), jnp.float32)

    def spread(c, which, at):
        return coef[c, which, pl.ds(at, GROUP, stride=0), :]

    def relax(source_ref, base, begin, end, unroll, store):

        @pl.loop(begin, end, step=unroll)
        def _(i):
            lines_at = [[source_ref[i + k, c] for c in range(cols)] for k in range(-1, unroll + 1)]
            for k in range(unroll):
                above, center, below = lines_at[k : k + 3]
                ahead = [pltpu.roll(v, 1, 1) for v in center]
                behind = [pltpu.roll(v, LANES - 1, 1) for v in center]
                for c in range(cols):
                    left = jnp.where(leftmost, ahead[c - 1] if c else nothing, ahead[c])
                    right = jnp.where(rightmost, behind[c + 1] if c + 1 < cols else nothing, behind[c])
                    laplace = below[c] + above[c] + right + left - 4.0 * center[c]
                    store(i + k, c, center[c] + spread(c, 0, base + i + k) * laplace)

    def keep(ref):
        def store(i, c, value):
            ref[i, c] = value
        return store

    def sweep(side, group, edge, store_last):
        span = half_rows + 2 * halo
        base = side * half_rows - halo + PAD
        for k in range(halo):
            at = half_rows - halo * side + k
            for c in range(cols):
                first[(half_rows + halo) * side + k, c] = nothing
                first[(half_rows + halo) * (1 - side) + k, c] = spread(c, 1, at + PAD) * edge(k, c, at)
        for c in range(cols):
            second[0, c] = nothing
            second[span - 1, c] = nothing

        @pl.loop(0, half_rows, step=LINES)
        def _(j):
            for k in range(LINES):
                at = half_rows * side + j + k
                for c in range(cols):
                    first[halo + j + k, c] = spread(c, 1, at + PAD) * line(c, group, at)

        relax(first, base, 1, span - 1, ROWS, keep(second))
        relax(second, base, 1, span - 1, ROWS, keep(first))
        relax(first, base, halo, span - halo, LINES, store_last)

    def sweep_tile(side, group, tile):
        begin = side * half_rows + tile * tile_rows - halo
        span = tile_rows + 2 * halo
        for k in range(span):
            at = begin + k
            for c in range(cols):
                first[k, c] = spread(c, 1, at + PAD) * line(c, group, lax.rem(at + height, height))
        for c in range(cols):
            second[0, c] = nothing
            second[span - 1, c] = nothing

        def store(i, c, value):
            at = pl.ds(aligned(group * GROUP, GROUP), GROUP)
            done[side * mid + tile, c, i - halo, at, :] = value

        base = begin + PAD
        relax(first, base, 1, span - 1, (span - 2) // 2, keep(second))
        relax(second, base, 1, span - 1, (span - 2) // 2, keep(first))
        relax(first, base, halo, span - halo, tile_rows, store)

    def sweep_own(side, group):
        def store(i, c, value):
            j = i - halo
            at = pl.ds(aligned(group * GROUP, GROUP), GROUP)
            done[side * mid + j // tile_rows, c, lax.rem(j, tile_rows), at, :] = value

        sweep(side, group, lambda k, c, at: line(c, group, at), store)

    def sweep_raw():
        def store(i, c, value):
            j = i - halo
            done_far[j // tile_rows, c, lax.rem(j, tile_rows), :, :] = value

        sweep(half, local // GROUP, lambda k, c, at: edge_in[k, c], store)

    groups = local // GROUP

    def rows_of(q):
        return pl.ds(q * part, part)

    def slots(at, count):
        return pl.ds(aligned(at, GROUP), count)

    fill_mix()

    wait_for(pair_tile, pair_recv)

    @pl.loop(1, near + 1)
    def _(i):
        to_row, to_col = in_half(i)
        remote(pair_tile, pair_tile, coef_send.at[2], far_recv, to_row, to_col).start()

    def tiles(count):
        return held.at[pl.ds(0, count), pl.ds(0, 2 * tile_rows)]

    wait_for(tiles(near), near_recv)
    wait_for(tiles(near), far_recv)

    own_slots = slots(source * local, local)

    def across(i):
        return other * mid + lax.rem(row + i // cols, mid), turn(i)

    def send_near(q):
        pltpu.make_async_copy(
            done.at[row, col, rows_of(q)], held.at[rows_of(q), own_slots], recv_sem.at[q]
        ).start()

        @pl.loop(1, near + 1)
        def _(i):
            to_row, to_col = in_half(near + 1 - i)
            remote(
                done.at[to_row, to_col, rows_of(q)], held.at[rows_of(q), own_slots],
                near_send, recv_sem.at[q], to_row, to_col,
            ).start()

    def cross_copy(q, skip, to_row, to_col):
        count = local - skip
        return remote(
            done.at[to_row, to_col, rows_of(q), pl.ds(skip, count)],
            held.at[rows_of(q), slots(source * local + skip, count)],
            cross_send, recv_sem.at[q], to_row, to_col,
        )

    def send_cross(q):
        @pl.loop(0, near + 1)
        def _(i):
            cross_copy(q, 0, *across(i)).start()

    @pl.when(raw)
    def _():
        @pl.loop(0, mid)
        def _(t):
            tile = lax.rem(row + t, mid)
            to_row = other * mid + tile

            @pl.loop(1, groups)
            def _(g):
                sweep_tile(other, g, tile)

            @pl.loop(0, steps)
            def _(q):
                @pl.loop(0, cols)
                def _(i):
                    cross_copy(q, GROUP, to_row, turn(i)).start()

    @pl.when(jnp.logical_not(raw))
    def _():
        @pl.loop(0, groups)
        def _(g):
            sweep_own(other, g)

    @pl.when(inner & jnp.logical_not(raw))
    def _():
        @pl.loop(0, steps)
        def _(q):
            send_cross(q)

    @pl.loop(0, groups)
    def _(g):
        sweep_own(half, g)

    @pl.loop(0, steps)
    def _(q):
        @pl.when(jnp.logical_not(inner))
        def _():
            send_cross(q)

        send_near(q)

    @pl.when(raw)
    def _():
        wait_for(x.at[:, local : local + GROUP, near_rows], raw_recv)
        edge_copy.wait_recv()
        sweep_raw()
        there = slots((mirror * cols + col) * local, GROUP)

        @pl.loop(0, steps)
        def _(q):
            pltpu.make_async_copy(
                done_far.at[row - half * mid, col, rows_of(q)], held.at[rows_of(q), there],
                recv_sem.at[q],
            ).start()

            @pl.loop(1, near + 1)
            def _(i):
                to_row, to_col = in_half(i)
                remote(
                    done_far.at[to_row - half * mid, to_col, rows_of(q)],
                    held.at[rows_of(q), there],
                    relay_send, recv_sem.at[q], to_row, to_col,
                ).start()

    @pl.loop(0, steps - 1)
    def _(q):
        wait_for(held.at[rows_of(q)], recv_sem.at[q])
        convolve(held, mix_ref, flux, q * part, part)

    wait_for(held.at[rows_of(steps - 1)], recv_sem.at[steps - 1])

    wait_for(own_tile, coef_send.at[0])
    wait_for(tiles(near), coef_send.at[1])
    wait_for(tiles(near), coef_send.at[2])
    wait_for(held.at[:, pl.ds(0, near * local)], near_send)

    @pl.when(raw)
    def _():
        wait_for(x.at[:, local : local + GROUP, far_rows], raw_send)
        edge_copy.wait_send()
        wait_for(held.at[:, pl.ds(0, (near + 1) * (local - GROUP))], cross_send)
        wait_for(held.at[:, pl.ds(0, near * GROUP)], relay_send)

    @pl.when(jnp.logical_not(raw))
    def _():
        wait_for(held.at[:, pl.ds(0, (near + 1) * local)], cross_send)


def convolve(held, mix_ref, flux, begin, count):
    total, width = held.shape[1], held.shape[2]
    x = jnp.transpose(held[pl.ds(begin, count)], (0, 2, 1)).reshape(count * width, total)
    high = x.astype(jnp.bfloat16)
    low = (x - high.astype(jnp.float32)).astype(jnp.bfloat16)
    cut = total // 2
    for a, b in ((0, cut), (cut, total)):
        out = jnp.dot(high[:, :b], mix_ref[0, :b, a:b], preferred_element_type=jnp.float32)
        out += jnp.dot(low[:, :b], mix_ref[0, :b, a:b], preferred_element_type=jnp.float32)
        out += jnp.dot(high[:, :b], mix_ref[1, :b, a:b], preferred_element_type=jnp.float32)
        flux[pl.ds(begin, count), :, a:b] = out.reshape(count, width, b - a)


def finish_kernel(part, held, flux, mix_ref, out, last, sem):
    rows = held.shape[0]
    ready = rows - part
    early = pltpu.make_async_copy(flux.at[0:ready], out.at[0:ready], sem.at[0])
    early.start()
    convolve(held.at[ready:rows], mix_ref, last, 0, part)
    late = pltpu.make_async_copy(last, out.at[ready:rows], sem.at[1])
    late.start()
    early.wait()
    late.wait()


def per_device(frames, class_index, surface_mask, effusivity, conductivity):
    rows = lax.axis_size("row")
    cols = lax.axis_size("col")
    local, height, width = frames.shape
    tile_rows, tile_cols = height // rows, width // cols
    total = local * rows * cols
    near = rows // 2 * cols - 1
    fits = (
        rows % 2 == 0 and cols % 2 == 0 and local % (2 * GROUP) == 0 and tile_rows % PAD == 0
        and tile_rows % STEPS == 0 and tile_cols == LANES and total % (2 * LANES) == 0
        and near <= tile_rows and cols >= EARLY and 2 * tile_rows <= total
        and height // 2 % LINES == 0 and (height // 2 + 2 * PASSES - 2) % ROWS == 0
    )
    if not fits:
        return plain_device(frames, class_index, surface_mask, effusivity, conductivity)
    half_rows, span = height // 2, height // 2 + 2 * PASSES
    vmem = pl.BlockSpec(memory_space=pltpu.VMEM)
    hbm = pl.BlockSpec(memory_space=pltpu.HBM)
    dma = pltpu.SemaphoreType.DMA
    f32 = jnp.float32
    arguments = (frames, class_index, surface_mask, effusivity, conductivity)
    held, flux, mix = pl.pallas_call(
        functools.partial(gather_kernel, rows, cols, tile_rows, tile_cols, local, height, STEPS),
        out_shape=(
            jax.ShapeDtypeStruct((tile_rows, total, LANES), f32),
            jax.ShapeDtypeStruct((tile_rows, tile_cols, total), f32),
            jax.ShapeDtypeStruct((2, total, total), jnp.bfloat16),
        ),
        in_specs=[hbm] * 5,
        out_specs=(vmem, vmem, vmem),
        scratch_shapes=[
            pltpu.VMEM((cols, local + 2 * GROUP, height, LANES), f32),
            pltpu.VMEM((cols, 2, height + 3 * PAD, LANES), f32),
            pltpu.VMEM((rows, cols, tile_rows, local, LANES), f32),
            pltpu.VMEM((rows // 2, cols, tile_rows, GROUP, LANES), f32),
            pltpu.VMEM((span, cols, GROUP, LANES), f32),
            pltpu.VMEM((span, cols, GROUP, LANES), f32),
            pltpu.VMEM((PASSES, cols, GROUP, LANES), f32),
            pltpu.VMEM((PASSES, cols, GROUP, LANES), f32),
            pltpu.VMEM((tile_rows, tile_cols), jnp.int32),
            pltpu.VMEM((tile_rows, tile_cols), jnp.int32),
            pltpu.SMEM(effusivity.shape, f32),
            pltpu.SMEM(conductivity.shape, f32),
            dma, dma((4,)), dma((3,)), dma, dma, dma,
            dma, dma, dma, dma,
            dma, dma, dma, dma((STEPS,)), pltpu.SemaphoreType.REGULAR,
        ],
        compiler_params=pltpu.CompilerParams(
            collective_id=0, has_side_effects=True, vmem_limit_bytes=VMEM_GATHER
        ),
        name="gather",
    )(*(pltpu.with_memory_space_constraint(a, pltpu.HBM) for a in arguments))
    part = tile_rows // STEPS
    return pl.pallas_call(
        functools.partial(finish_kernel, part),
        out_shape=jax.ShapeDtypeStruct((tile_rows, tile_cols, total), f32),
        in_specs=[vmem, vmem, vmem],
        out_specs=hbm,
        scratch_shapes=[pltpu.VMEM((part, tile_cols, total), f32), dma((2,))],
        compiler_params=pltpu.CompilerParams(vmem_limit_bytes=24 * 2**20),
        name="finish",
    )(held, flux, mix)


def solution(mesh):
    in_specs = (P(("row", "col"), None, None), P("row", "col"), P("row", "col"), P(), P())
    out_specs = P("row", "col", None)
    return jax.shard_map(
        per_device, mesh=mesh, in_specs=in_specs, out_specs=out_specs, check_vma=False
    )
```

```python
import functools
import jax
import jax.numpy as jnp
from jax import lax
from jax.experimental import pallas as pl
from jax.experimental.pallas import tpu as pltpu
from jax.sharding import PartitionSpec as P

PASSES = 3
PAD = 8
GROUP = 8
LANES = 128
STEPS = 4
ROWS = 12
LINES = 16
EARLY = 1
VMEM_GATHER = 40 * 2**20
MESH = pl.DeviceIdType.MESH

flux_factor = 1.1283791670955126
lateral_rate = 0.24


def extended(block, sides, width):
    for axis, dim in sides:
        count = lax.axis_size(axis)
        forward = [(i, i + 1) for i in range(count - 1)]
        backward = [(target, source) for source, target in forward]
        low = lax.ppermute(
            lax.slice_in_dim(block, block.shape[dim] - width, None, axis=dim), axis, forward
        )
        high = lax.ppermute(lax.slice_in_dim(block, 0, width, axis=dim), axis, backward)
        block = jnp.concatenate([low, block, high], axis=dim)
    return block


def weights(lagged):
    clipped = jnp.maximum(lagged, 0.0)
    return jnp.where(lagged >= 0.0, 1.0 / (jnp.sqrt(clipped) + jnp.sqrt(clipped + 1.0)), 0.0)


def kernel_from(later, earlier):
    lagged = (later[:, None] - earlier[None, :]).astype(jnp.float32)
    return weights(lagged) - weights(lagged - 1.0)


def relax_once(padded, lateral):
    center = padded[1:-1, 1:-1]
    laplace = (
        padded[2:, 1:-1] + padded[:-2, 1:-1] + padded[1:-1, 2:] + padded[1:-1, :-2] - 4.0 * center
    )
    return center + lateral[:, :, None] * laplace


def plain_device(frames, class_index, surface_mask, effusivity, conductivity):
    row_count = lax.axis_size("row")
    col_count = lax.axis_size("col")
    local_frames, height, width = frames.shape
    tile_rows = height // row_count
    tile_cols = width // col_count
    total_frames = local_frames * row_count * col_count
    frame_ids = jnp.arange(total_frames, dtype=jnp.int32)
    contract = (((0,), (1,)), ((), ()))
    kernel = kernel_from(frame_ids, frame_ids)
    blocks = frames.reshape(local_frames, row_count, tile_rows, col_count, tile_cols)
    blocks = blocks.transpose(0, 1, 3, 2, 4).reshape(
        local_frames, row_count * col_count, tile_rows, tile_cols
    )
    convolved = lax.dot_general(
        lax.all_to_all(blocks, ("row", "col"), split_axis=1, concat_axis=0, tiled=True)[:, 0],
        kernel,
        contract,
        precision=lax.Precision.HIGHEST,
    )
    classes = jnp.arange(effusivity.shape[0], dtype=jnp.int32)
    matches = (class_index[:, :, None] == classes[None, None, :]).astype(jnp.float32)
    maskf = surface_mask.astype(jnp.float32)
    gain = flux_factor * jnp.sum(matches * effusivity, axis=-1) * maskf
    lateral = lateral_rate * jnp.sum(matches * conductivity, axis=-1) * maskf
    heat_flux = convolved * gain[:, :, None]
    padded = extended(heat_flux, (("row", 0), ("col", 1)), PASSES)
    lateral_wide = extended(lateral, (("row", 0), ("col", 1)), PASSES - 1)
    for pass_index in range(PASSES):
        margin = PASSES - 1 - pass_index
        offset = PASSES - 1 - margin
        lateral_part = lateral_wide[
            offset : offset + tile_rows + 2 * margin, offset : offset + tile_cols + 2 * margin
        ]
        padded = relax_once(padded, lateral_part)
    return padded


def gather_kernel(
    rows, cols, tile_rows, tile_cols, local, height, steps,
    frames, class_in, mask_in, eff_in, cond_in,
    held, flux, mix_ref,
    x, coef, done, done_far, first, second, edge_out, edge_in,
    class_ref, mask_ref, eff_ref, cond_ref,
    load_sem, small_sem, coef_send, near_recv, pair_recv, far_recv,
    raw_send, raw_recv, edge_send, edge_recv,
    near_send, cross_send, relay_send, recv_sem, ready,
):
    row, col = lax.axis_index("row"), lax.axis_index("col")
    mid = rows // 2
    half = row // mid
    other = 1 - half
    half_rows = height // 2
    total = rows * cols * local
    halo = PASSES
    near = mid * cols - 1
    part = tile_rows // steps
    source = row * cols + col
    mirror, pair = rows - 1 - row, lax.rem(row + mid, rows)
    inner = (row == mid - 1) | (row == mid)
    raw = inner & (lax.rem(col, 2) == 0)

    def wait_for(ref, sem):
        pltpu.make_async_copy(ref, ref, sem).wait()

    def aligned(value, unit):
        return pl.multiple_of(value, unit)

    def remote(src, dst, send, recv, to_row, to_col):
        return pltpu.make_async_remote_copy(
            src_ref=src, dst_ref=dst, send_sem=send, recv_sem=recv,
            device_id=(to_row, to_col), device_id_type=MESH,
        )

    def turn(i):
        return lax.rem(col + lax.rem(i, cols // 2) * 2 + lax.rem(i // (cols // 2), 2), cols)

    def in_half(i):
        return half * mid + lax.rem(row + i // cols, mid), lax.rem(col + i, cols)

    barrier = pltpu.get_barrier_semaphore()

    def greet(to_row, to_col):
        pl.semaphore_signal(barrier, inc=1, device_id=(to_row, to_col), device_id_type=MESH)

    def is_inner(at_row):
        return (at_row == mid - 1) | (at_row == mid)

    @pl.when(raw)
    def _():
        greet(mirror, col)

    even = lax.rem(col, 2) == 0
    greet(pair, col + (is_inner(pair) & even).astype(jnp.int32))

    @pl.loop(1, near + 1)
    def _(i):
        to_row, to_col = in_half(i)

        @pl.when(jnp.logical_not(is_inner(to_row) & (lax.rem(to_col, 2) == 0)))
        def _():
            greet(to_row, to_col)

    smalls = [
        pltpu.make_async_copy(src, dst, small_sem.at[i])
        for i, (src, dst) in enumerate(
            ((class_in, class_ref), (mask_in, mask_ref), (eff_in, eff_ref), (cond_in, cond_ref))
        )
    ]
    for copy in smalls:
        copy.start()
    for c in range(cols):
        pltpu.make_async_copy(
            frames.at[:, :, c * LANES : (c + 1) * LANES], x.at[c, 0:local], load_sem
        ).start()

    proxy = inner & jnp.logical_not(even)

    far_rows = pl.ds(aligned(other * half_rows, PAD), half_rows)
    near_rows = pl.ds(aligned(half * half_rows, PAD), half_rows)

    def raw_copy(c):
        return remote(
            frames.at[0:GROUP, far_rows, c * LANES : (c + 1) * LANES],
            x.at[c, local : local + GROUP, far_rows],
            raw_send, raw_recv, mirror, col,
        )

    @pl.when(raw)
    def _():
        pl.semaphore_wait(barrier, 1)
        for c in range(EARLY):
            raw_copy(c).start()

    for copy in smalls:
        copy.wait()
    classes = class_ref[...]
    maskf = mask_ref[...].astype(jnp.float32)
    eff = jnp.zeros(classes.shape, jnp.float32)
    cond = jnp.zeros(classes.shape, jnp.float32)
    for k in range(eff_ref.shape[0]):
        eff = jnp.where(classes == k, eff_ref[k], eff)
        cond = jnp.where(classes == k, cond_ref[k], cond)

    def tile_of(at_row, at_col):
        return coef.at[at_col, :, pl.ds(aligned(PAD + at_row * tile_rows, PAD), tile_rows)]

    own_rows = pl.ds(aligned(PAD + row * tile_rows, PAD), tile_rows)
    coef[col, 0, own_rows] = lateral_rate * cond * maskf
    coef[col, 1, own_rows] = flux_factor * eff * maskf
    for c in range(cols):
        for k in range(2):
            coef[c, k, 0:PAD] = jnp.zeros((PAD, LANES), jnp.float32)
            coef[c, k, PAD + height : 2 * PAD + height] = jnp.zeros((PAD, LANES), jnp.float32)

    @pl.when(jnp.logical_not(raw))
    def _():
        pl.semaphore_wait(barrier, near + 1 + proxy.astype(jnp.int32))

    @pl.when(proxy)
    def _():
        pl.semaphore_signal(ready, inc=1, device_id=(row, col - 1), device_id_type=MESH)

    @pl.when(raw)
    def _():
        pl.semaphore_wait(ready, 1)


    own_tile, pair_tile = tile_of(row, col), tile_of(pair, col)
    remote(own_tile, own_tile, coef_send.at[0], pair_recv, pair, col).start()

    @pl.loop(1, near + 1)
    def _(i):
        to_row, to_col = in_half(i)
        remote(own_tile, own_tile, coef_send.at[1], near_recv, to_row, to_col).start()

    edge_copy = remote(edge_out, edge_in, edge_send, edge_recv, mirror, col)

    @pl.when(raw)
    def _():
        for c in range(EARLY, cols):
            raw_copy(c).start()

    wait_for(x.at[:, 0:local], load_sem)
    lines = x.reshape(cols, x.shape[1] * height, LANES)

    def line(c, group, at):
        return lines[c, pl.ds(group * (GROUP * height) + at, GROUP, stride=height), :]

    @pl.when(raw)
    def _():
        for k in range(halo):
            for c in range(cols):
                edge_out[k, c] = line(c, 0, half_rows - halo * other + k)
        edge_copy.start()

    def fill_mix():
        block = tile_cols

        @pl.loop(0, total // block)
        def _(k):
            shape = (block, total)
            earlier = lax.broadcasted_iota(jnp.int32, shape, 0) + k * block
            later = lax.broadcasted_iota(jnp.int32, shape, 1)
            lagged = (later - earlier).astype(jnp.float32)
            mix = weights(lagged) - weights(lagged - 1.0)
            high = mix.astype(jnp.bfloat16)
            at = pl.ds(aligned(k * block, block), block)
            mix_ref[0, at] = high
            mix_ref[1, at] = (mix - high.astype(jnp.float32)).astype(jnp.bfloat16)

    lane = lax.broadcasted_iota(jnp.int32, (GROUP, LANES), 1)
    leftmost, rightmost = lane == 0, lane == LANES - 1
    nothing = jnp.zeros((GROUP, LANES), jnp.float32)

    def spread(c, which, at):
        return coef[c, which, pl.ds(at, GROUP, stride=0), :]

    def relax(source_ref, base, begin, end, unroll, store):

        @pl.loop(begin, end, step=unroll)
        def _(i):
            lines_at = [[source_ref[i + k, c] for c in range(cols)] for k in range(-1, unroll + 1)]
            for k in range(unroll):
                above, center, below = lines_at[k : k + 3]
                ahead = [pltpu.roll(v, 1, 1) for v in center]
                behind = [pltpu.roll(v, LANES - 1, 1) for v in center]
                for c in range(cols):
                    left = jnp.where(leftmost, ahead[c - 1] if c else nothing, ahead[c])
                    right = jnp.where(rightmost, behind[c + 1] if c + 1 < cols else nothing, behind[c])
                    laplace = below[c] + above[c] + right + left - 4.0 * center[c]
                    store(i + k, c, center[c] + spread(c, 0, base + i + k) * laplace)

    def keep(ref):
        def store(i, c, value):
            ref[i, c] = value
        return store

    def sweep(side, group, edge, store_last):
        span = half_rows + 2 * halo
        base = side * half_rows - halo + PAD
        for k in range(halo):
            at = half_rows - halo * side + k
            for c in range(cols):
                first[(half_rows + halo) * side + k, c] = nothing
                first[(half_rows + halo) * (1 - side) + k, c] = spread(c, 1, at + PAD) * edge(k, c, at)
        for c in range(cols):
            second[0, c] = nothing
            second[span - 1, c] = nothing

        @pl.loop(0, half_rows, step=LINES)
        def _(j):
            for k in range(LINES):
                at = half_rows * side + j + k
                for c in range(cols):
                    first[halo + j + k, c] = spread(c, 1, at + PAD) * line(c, group, at)

        relax(first, base, 1, span - 1, ROWS, keep(second))
        relax(second, base, 1, span - 1, ROWS, keep(first))
        relax(first, base, halo, span - halo, LINES, store_last)

    def sweep_tile(side, group, tile):
        begin = side * half_rows + tile * tile_rows - halo
        span = tile_rows + 2 * halo
        for k in range(span):
            at = begin + k
            for c in range(cols):
                first[k, c] = spread(c, 1, at + PAD) * line(c, group, lax.rem(at + height, height))
        for c in range(cols):
            second[0, c] = nothing
            second[span - 1, c] = nothing

        def store(i, c, value):
            at = pl.ds(aligned(group * GROUP, GROUP), GROUP)
            done[side * mid + tile, c, i - halo, at, :] = value

        base = begin + PAD
        relax(first, base, 1, span - 1, (span - 2) // 2, keep(second))
        relax(second, base, 1, span - 1, (span - 2) // 2, keep(first))
        relax(first, base, halo, span - halo, tile_rows, store)

    def sweep_own(side, group):
        def store(i, c, value):
            j = i - halo
            at = pl.ds(aligned(group * GROUP, GROUP), GROUP)
            done[side * mid + j // tile_rows, c, lax.rem(j, tile_rows), at, :] = value

        sweep(side, group, lambda k, c, at: line(c, group, at), store)

    def sweep_raw():
        def store(i, c, value):
            j = i - halo
            done_far[j // tile_rows, c, lax.rem(j, tile_rows), :, :] = value

        sweep(half, local // GROUP, lambda k, c, at: edge_in[k, c], store)

    groups = local // GROUP

    def rows_of(q):
        return pl.ds(q * part, part)

    def slots(at, count):
        return pl.ds(aligned(at, GROUP), count)

    fill_mix()

    wait_for(pair_tile, pair_recv)

    @pl.loop(1, near + 1)
    def _(i):
        to_row, to_col = in_half(i)
        remote(pair_tile, pair_tile, coef_send.at[2], far_recv, to_row, to_col).start()

    def tiles(count):
        return held.at[pl.ds(0, count), pl.ds(0, 2 * tile_rows)]

    wait_for(tiles(near), near_recv)
    wait_for(tiles(near), far_recv)

    own_slots = slots(source * local, local)

    def across(i):
        return other * mid + lax.rem(row + i // cols, mid), turn(i)

    def send_near(q):
        pltpu.make_async_copy(
            done.at[row, col, rows_of(q)], held.at[rows_of(q), own_slots], recv_sem.at[q]
        ).start()

        @pl.loop(1, near + 1)
        def _(i):
            to_row, to_col = in_half(near + 1 - i)
            remote(
                done.at[to_row, to_col, rows_of(q)], held.at[rows_of(q), own_slots],
                near_send, recv_sem.at[q], to_row, to_col,
            ).start()

    def cross_copy(q, skip, to_row, to_col):
        count = local - skip
        return remote(
            done.at[to_row, to_col, rows_of(q), pl.ds(skip, count)],
            held.at[rows_of(q), slots(source * local + skip, count)],
            cross_send, recv_sem.at[q], to_row, to_col,
        )

    def send_cross(q):
        @pl.loop(0, near + 1)
        def _(i):
            cross_copy(q, 0, *across(i)).start()

    @pl.when(raw)
    def _():
        @pl.loop(0, mid)
        def _(t):
            tile = lax.rem(row + t, mid)
            to_row = other * mid + tile

            @pl.loop(1, groups)
            def _(g):
                sweep_tile(other, g, tile)

            @pl.loop(0, steps)
            def _(q):
                @pl.loop(0, cols)
                def _(i):
                    cross_copy(q, GROUP, to_row, turn(i)).start()

    @pl.when(jnp.logical_not(raw))
    def _():
        @pl.loop(0, groups)
        def _(g):
            sweep_own(other, g)

    @pl.when(inner & jnp.logical_not(raw))
    def _():
        @pl.loop(0, steps)
        def _(q):
            send_cross(q)

    @pl.when(jnp.logical_not(inner))
    def _():
        send_cross(0)

    @pl.loop(0, groups)
    def _(g):
        sweep_own(half, g)

    @pl.loop(0, steps)
    def _(q):
        @pl.when(jnp.logical_not(inner) & (q > 0))
        def _():
            send_cross(q)

        send_near(q)

    @pl.when(raw)
    def _():
        wait_for(x.at[:, local : local + GROUP, near_rows], raw_recv)
        edge_copy.wait_recv()
        sweep_raw()
        there = slots((mirror * cols + col) * local, GROUP)

        @pl.loop(0, steps)
        def _(q):
            pltpu.make_async_copy(
                done_far.at[row - half * mid, col, rows_of(q)], held.at[rows_of(q), there],
                recv_sem.at[q],
            ).start()

            @pl.loop(1, near + 1)
            def _(i):
                to_row, to_col = in_half(i)
                remote(
                    done_far.at[to_row - half * mid, to_col, rows_of(q)],
                    held.at[rows_of(q), there],
                    relay_send, recv_sem.at[q], to_row, to_col,
                ).start()

    @pl.loop(0, steps - 1)
    def _(q):
        wait_for(held.at[rows_of(q)], recv_sem.at[q])
        convolve(held, mix_ref, flux, q * part, part)

    wait_for(held.at[rows_of(steps - 1)], recv_sem.at[steps - 1])

    wait_for(own_tile, coef_send.at[0])
    wait_for(tiles(near), coef_send.at[1])
    wait_for(tiles(near), coef_send.at[2])
    wait_for(held.at[:, pl.ds(0, near * local)], near_send)

    @pl.when(raw)
    def _():
        wait_for(x.at[:, local : local + GROUP, far_rows], raw_send)
        edge_copy.wait_send()
        wait_for(held.at[:, pl.ds(0, (near + 1) * (local - GROUP))], cross_send)
        wait_for(held.at[:, pl.ds(0, near * GROUP)], relay_send)

    @pl.when(jnp.logical_not(raw))
    def _():
        wait_for(held.at[:, pl.ds(0, (near + 1) * local)], cross_send)


def convolve(held, mix_ref, flux, begin, count):
    total, width = held.shape[1], held.shape[2]
    x = jnp.transpose(held[pl.ds(begin, count)], (0, 2, 1)).reshape(count * width, total)
    high = x.astype(jnp.bfloat16)
    low = (x - high.astype(jnp.float32)).astype(jnp.bfloat16)
    cut = total // 2
    for a, b in ((0, cut), (cut, total)):
        out = jnp.dot(high[:, :b], mix_ref[0, :b, a:b], preferred_element_type=jnp.float32)
        out += jnp.dot(low[:, :b], mix_ref[0, :b, a:b], preferred_element_type=jnp.float32)
        out += jnp.dot(high[:, :b], mix_ref[1, :b, a:b], preferred_element_type=jnp.float32)
        flux[pl.ds(begin, count), :, a:b] = out.reshape(count, width, b - a)


def finish_kernel(part, held, flux, mix_ref, out, last, sem):
    rows = held.shape[0]
    ready = rows - part
    early = pltpu.make_async_copy(flux.at[0:ready], out.at[0:ready], sem.at[0])
    early.start()
    convolve(held.at[ready:rows], mix_ref, last, 0, part)
    late = pltpu.make_async_copy(last, out.at[ready:rows], sem.at[1])
    late.start()
    early.wait()
    late.wait()


def per_device(frames, class_index, surface_mask, effusivity, conductivity):
    rows = lax.axis_size("row")
    cols = lax.axis_size("col")
    local, height, width = frames.shape
    tile_rows, tile_cols = height // rows, width // cols
    total = local * rows * cols
    near = rows // 2 * cols - 1
    fits = (
        rows % 2 == 0 and cols % 2 == 0 and local % (2 * GROUP) == 0 and tile_rows % PAD == 0
        and tile_rows % STEPS == 0 and tile_cols == LANES and total % (2 * LANES) == 0
        and near <= tile_rows and cols >= EARLY and 2 * tile_rows <= total
        and height // 2 % LINES == 0 and (height // 2 + 2 * PASSES - 2) % ROWS == 0
    )
    if not fits:
        return plain_device(frames, class_index, surface_mask, effusivity, conductivity)
    half_rows, span = height // 2, height // 2 + 2 * PASSES
    vmem = pl.BlockSpec(memory_space=pltpu.VMEM)
    hbm = pl.BlockSpec(memory_space=pltpu.HBM)
    dma = pltpu.SemaphoreType.DMA
    f32 = jnp.float32
    arguments = (frames, class_index, surface_mask, effusivity, conductivity)
    held, flux, mix = pl.pallas_call(
        functools.partial(gather_kernel, rows, cols, tile_rows, tile_cols, local, height, STEPS),
        out_shape=(
            jax.ShapeDtypeStruct((tile_rows, total, LANES), f32),
            jax.ShapeDtypeStruct((tile_rows, tile_cols, total), f32),
            jax.ShapeDtypeStruct((2, total, total), jnp.bfloat16),
        ),
        in_specs=[hbm] * 5,
        out_specs=(vmem, vmem, vmem),
        scratch_shapes=[
            pltpu.VMEM((cols, local + 2 * GROUP, height, LANES), f32),
            pltpu.VMEM((cols, 2, height + 3 * PAD, LANES), f32),
            pltpu.VMEM((rows, cols, tile_rows, local, LANES), f32),
            pltpu.VMEM((rows // 2, cols, tile_rows, GROUP, LANES), f32),
            pltpu.VMEM((span, cols, GROUP, LANES), f32),
            pltpu.VMEM((span, cols, GROUP, LANES), f32),
            pltpu.VMEM((PASSES, cols, GROUP, LANES), f32),
            pltpu.VMEM((PASSES, cols, GROUP, LANES), f32),
            pltpu.VMEM((tile_rows, tile_cols), jnp.int32),
            pltpu.VMEM((tile_rows, tile_cols), jnp.int32),
            pltpu.SMEM(effusivity.shape, f32),
            pltpu.SMEM(conductivity.shape, f32),
            dma, dma((4,)), dma((3,)), dma, dma, dma,
            dma, dma, dma, dma,
            dma, dma, dma, dma((STEPS,)), pltpu.SemaphoreType.REGULAR,
        ],
        compiler_params=pltpu.CompilerParams(
            collective_id=0, has_side_effects=True, vmem_limit_bytes=VMEM_GATHER
        ),
        name="gather",
    )(*(pltpu.with_memory_space_constraint(a, pltpu.HBM) for a in arguments))
    part = tile_rows // STEPS
    return pl.pallas_call(
        functools.partial(finish_kernel, part),
        out_shape=jax.ShapeDtypeStruct((tile_rows, tile_cols, total), f32),
        in_specs=[vmem, vmem, vmem],
        out_specs=hbm,
        scratch_shapes=[pltpu.VMEM((part, tile_cols, total), f32), dma((2,))],
        compiler_params=pltpu.CompilerParams(vmem_limit_bytes=24 * 2**20),
        name="finish",
    )(held, flux, mix)


def solution(mesh):
    in_specs = (P(("row", "col"), None, None), P("row", "col"), P("row", "col"), P(), P())
    out_specs = P("row", "col", None)
    return jax.shard_map(
        per_device, mesh=mesh, in_specs=in_specs, out_specs=out_specs, check_vma=False
    )
```
